256 devices in a mesh: worker: 16 (over z_hi, x), tok: 16 (over z_lo, y, core).
Axes of the slice: x: 4, y: 4, z: 8 (z_hi: 4, z_lo: 2; z = z_hi * 2 + z_lo), core: 2. Of those that a mesh axis runs over, the one named last changes fastest.
Arguments:
- inputs: bfloat16 [16, 24576, 2048], P('worker', 'tok'), may hold values from -6 to 6
- cotangent: bfloat16 [16, 24576, 1024], P('worker', 'tok'), may hold values from -0.038085938 to 0.038085938
- weights: float32 [16, 2048, 1024], P('worker', 'tok'), may hold values from -12 to 12
- momentum: float32 [16, 2048, 1024], P('worker', 'tok'), may hold values from -6 to 6
- mix_weights: int32 [16, 5], P('worker'), may hold values from 1 to 5
- clip_radius: int32 [2], replicated, may hold values from 700 to 2299
Outputs:
- new_weights: float32 [16, 2048, 1024], P('worker', 'tok')
- new_momentum: float32 [16, 2048, 1024], P('worker', 'tok')
The draws below stay inside these ranges and needn't reach their ends.
All inputs are finite; a program needn't handle non-finite values.
Results may differ from the reference program's by a relative error of at most 0.0003.
Values sent between devices are 32-bit elements; how exact they have to be, the bound alone decides.
A program may use at most 64 MiB of HBM per device.

```python
import math
import jax
import jax.numpy as jnp
from jax import lax

D = 2048
KV_WIDTH = 512
ROUNDS = 2
TOKENS = 24576
WORKERS = 16


def draw_weights(key, part):
    base_key = jax.random.fold_in(key, 11)
    scale_key, entry_key = jax.random.split(base_key, 2)
    shape = (WORKERS, D, 2 * KV_WIDTH)
    worker_scale = jnp.exp(jax.random.uniform(scale_key, (WORKERS, 1, 1), jnp.float32, jnp.log(0.25), 0.0))
    row_scale = (1.0 + 2.0 * jnp.arange(D, dtype=jnp.float32) / (D - 1)).reshape(1, D, 1)
    entries = jax.random.truncated_normal(entry_key, -4.0, 4.0, shape, jnp.float32)
    return (entries * worker_scale * row_scale).astype(jnp.float32)


def touch_ends(values, key, low, largest):
    longest = values.shape.index(max(values.shape))
    spots = []
    for shift in (0, 1):
        where = [jax.random.randint(jax.random.fold_in(key, axis), (), 0, length) for axis, length in enumerate(values.shape)]
        where[longest] = (where[longest] + shift) % values.shape[longest]
        spots.append(tuple(where))
    return values.at[spots[0]].set(low).at[spots[1]].set(largest)


def block_levels(own_key, extent, cuts, low, high):
    loudness, own = 1.0, jax.random.fold_in(own_key, 6)
    for dim, shards_of in cuts:
        steps = jnp.exp(jax.random.uniform(jax.random.fold_in(own, dim), (shards_of,), jnp.float32, low / len(cuts), high / len(cuts)))
        loudness = loudness * jnp.repeat(steps, extent[dim] // shards_of).reshape([-1 if axis == dim else 1 for axis in range(len(extent))])
    return loudness


def scatter_about(key, dims, scale, limit, pieces=(), kind=jnp.bfloat16):
    drawn = jax.random.normal(key, dims, jnp.float32) * scale
    if len(pieces) > 0:
        drawn = block_levels(key, dims, pieces, -0.22, 0.18) * drawn
    return jnp.clip(drawn, min=-limit, max=limit).astype(kind)


def setup_inputs(seed: int = 0) -> dict:
    key_of = jax.random.split(jax.random.key(seed), 7)
    return {
        "inputs": scatter_about(key_of[0], (WORKERS, TOKENS, D), 1.0, 6.0, ((0, 16), (1, 16))),
        "cotangent": scatter_about(key_of[1], (WORKERS, TOKENS, 2 * KV_WIDTH), (TOKENS ** -0.5), 0.038085938, ((0, 16), (1, 16))),
        "weights": draw_weights(jax.random.fold_in(key_of[6], 71), 0),
        "momentum": scatter_about(key_of[3], (WORKERS, D, 2 * KV_WIDTH), 1.0, 6.0, ((0, 16), (1, 16)), jnp.float32),
        "mix_weights": touch_ends(jax.random.randint(key_of[4], (WORKERS, 5), 1, 6), jax.random.fold_in(key_of[4], 1), 1, 5).astype(jnp.int32),
        "clip_radius": jax.random.randint(key_of[5], (ROUNDS,), 700, 2300).astype(jnp.int32),
    }


LEARNING_RATE = 0.25

def reference(inputs, cotangent, weights, momentum, mix_weights, clip_radius):

    def worker_gradient(pair):
        features, upstream = pair
        return lax.dot_general(features, upstream, (((0,), (0,)), ((), ())), preferred_element_type=jnp.float32)
    gradient = lax.map(worker_gradient, (inputs, cotangent))
    velocity = 0.5 * momentum + gradient
    current = weights - LEARNING_RATE * velocity
    mixing = mix_weights.astype(jnp.float32)
    shares = mixing / lax.optimization_barrier(jnp.sum(mixing, axis=1, keepdims=True))
    radius_all = clip_radius.astype(jnp.float32) * (math.sqrt(D * KV_WIDTH) / 1000.0)
    worker_ids = jnp.arange(WORKERS, dtype=jnp.int32)
    neighbour_ids = [worker_ids ^ 1, worker_ids ^ 2, (worker_ids - 4) % WORKERS, (worker_ids + 4) % WORKERS]
    for round_index in range(ROUNDS):
        radius = radius_all[round_index]
        mixed_step = jnp.zeros((WORKERS, D, 2, KV_WIDTH), jnp.float32)
        for position, peer_ids in enumerate(neighbour_ids):
            difference = current[peer_ids] - current
            halves = difference.reshape(WORKERS, D, 2, KV_WIDTH)
            distance = jnp.sqrt(lax.optimization_barrier(jnp.sum(halves * halves, axis=(1, 3))))
            factor = radius / jnp.maximum(distance, radius)
            scaled = halves * (shares[:, position + 1][:, None] * factor)[:, None, :, None]
            mixed_step = mixed_step + scaled
        current = current + mixed_step.reshape(current.shape)
    return (current, velocity)
```

```python
import math

import jax
import jax.numpy as jnp
from jax import lax
from jax.experimental import pallas as pl
from jax.experimental.pallas import tpu as pltpu
from jax.sharding import PartitionSpec as P

D = 2048
KV_WIDTH = 512
ROUNDS = 2
LEARNING_RATE = 0.25

MESH = pl.DeviceIdType.MESH
F32 = jnp.float32
BF16 = jnp.bfloat16
HIGHEST = lax.Precision.HIGHEST

ORDER = ((1, 2), (0, 2), (1, 1), (1, 3), (1, 0), (0, 1), (0, 3), (0, 0))
PAIRS = 3


def kernel(
    feat, cot, wts, mom, mix, clip, o_new, o_vel,
    F, C, PA, PR, Y1, Y2, ZR, ZF, W1, W2, WT, MO, CUR, RX, NEW, NR, DP, PAY, R1, R2, MS, MR, KC,
    ld, d_s, d_r, y1_s, y1_r, y2_s, y2_r, z_s, z_r, zf_s, zf_r, w1_s, w1_r, w2_s, w2_r,
    a_s, a_r, m_s, m_r, r_s, r_r, b_s, b_r,
):
    t = lax.axis_index("tok")
    w = lax.axis_index("worker")
    q, y, c = t // 8, (t // 2) % 4, t % 2
    flip = (1 - q) * 8 + y * 2 + c
    sibling = {"worker": w, "tok": q * 8 + y * 2 + (1 - c)}
    up = {"worker": w, "tok": q * 8 + lax.rem(y + 1, 4) * 2 + c}
    down = {"worker": w, "tok": q * 8 + lax.rem(y + 3, 4) * 2 + c}
    across = {"worker": w, "tok": flip}
    tok_peers = [{"worker": w, "tok": lax.rem(t + i, 16)} for i in range(1, 16)]
    work_peers = [{"worker": lax.rem(w + i, 16), "tok": flip} for i in range(1, 16)]

    barrier = pltpu.get_barrier_semaphore()
    for peer in tok_peers + work_peers:
        pl.semaphore_signal(barrier, inc=1, device_id=peer, device_id_type=MESH)

    def load(src, dst, i):
        cp = pltpu.make_async_copy(src, dst, ld.at[i])
        cp.start()
        return cp

    def send(src, dst, ss, rs, peer):
        cp = pltpu.make_async_remote_copy(
            src_ref=src, dst_ref=dst, send_sem=ss, recv_sem=rs, device_id=peer, device_id_type=MESH
        )
        cp.start()
        return cp

    def wait_bytes(ref, sem):
        pltpu.make_async_copy(ref, ref, sem).wait()

    def feat_block(j):
        dq, dy = ORDER[j]
        chip = (q + dq) % 2 * 4 + lax.rem(y + dy, 4)
        return feat.at[:, pl.ds(pl.multiple_of(chip * 256, 256), 256)]

    f_loads = [load(feat_block(0), F.at[0], 0)]
    c_loads = [load(cot.at[:, n * 256 : (n + 1) * 256], C.at[n], 8 + n) for n in range(4)]
    f_loads += [load(feat_block(j), F.at[j], j) for j in range(1, 8)]
    w_load, m_load = load(wts, WT, 12), load(mom, MO, 13)

    MS[...] = jnp.zeros_like(MS)
    MS[0:1, 0:5] = mix[...].astype(F32)
    MR[w] = MS[...]
    for half in range(2):
        for i in range(16):
            DP[half * 256 + i * 17 : half * 256 + i * 17 + 1, :] = jnp.zeros((1, 128), F32)

    sends = []

    def multiply(j):
        dq, dy = ORDER[j]
        f_loads[j].wait()
        if j == 0:
            for cp in c_loads:
                cp.wait()

        def columns(n, _):
            r = lax.dot_general(F[j], C[n], (((0,), (0,)), ((), ())), preferred_element_type=F32)
            for core in range(2):
                for k in range(2):
                    PA[core, dq, dy, 2 * n + k] = r[core * 128 : core * 128 + 128, k * 128 : k * 128 + 128]
            return 0

        lax.fori_loop(0, 4, columns, 0)

    mine = PA.at[c]

    def to_sibling(j):
        dq, dy = ORDER[j]
        return send(PA.at[1 - c, dq, dy], PR.at[dq, dy], d_s.at[j], d_r.at[j], sibling)

    def add_sibling(j, cp):
        dq, dy = ORDER[j]
        cp.wait_recv()
        mine[dq, dy] = mine[dq, dy] + PR[dq, dy]

    multiply(0)
    pl.semaphore_wait(barrier, 30)
    d = [to_sibling(0)]
    for peer in work_peers:
        send(MS, MR.at[w], m_s.at[0], m_r.at[0], peer)

    zf, y1 = {}, {}

    def first_across(dy):
        zf[dy] = send(mine.at[1, dy, 6:8], ZF.at[dy], zf_s.at[dy], zf_r.at[dy], across)

    for j in range(1, 8):
        multiply(j)
        d.append(to_sibling(j))
        add_sibling(j - 1, d[j - 1])
        if j == 2:
            for k in range(6):
                y1[k] = send(mine.at[:, 2, k], Y1.at[k], y1_s.at[k], y1_r.at[k], (up, down)[k % 2])
            first_across(2)
        if 3 <= j <= 5:
            first_across(ORDER[j - 1][1])
    add_sibling(7, d[7])

    y2 = {}

    def second(p):
        a, b = 2 * p, 2 * p + 1
        y1[a].wait_recv()
        mine[:, 1, a] = mine[:, 1, a] + Y1[a]
        y2[0, a] = send(mine.at[:, 1, a], Y2.at[0, a], y2_s.at[0, a], y2_r.at[0, a], up)
        y1[b].wait_recv()
        mine[:, 3, b] = mine[:, 3, b] + Y1[b]
        y2[1, b] = send(mine.at[:, 3, b], Y2.at[1, b], y2_s.at[1, b], y2_r.at[1, b], down)
        y2[0, b] = send(mine.at[:, 1, b], Y2.at[0, b], y2_s.at[0, b], y2_r.at[0, b], up)
        y2[1, a] = send(mine.at[:, 3, a], Y2.at[1, a], y2_s.at[1, a], y2_r.at[1, a], down)

    z = {}

    def own(p):
        for k in (2 * p, 2 * p + 1):
            y2[0, k].wait_recv()
            y2[1, k].wait_recv()
            mine[:, 0, k] = mine[:, 0, k] + Y2[0, k] + Y2[1, k]
        z[p] = send(mine.at[1, 0, 2 * p : 2 * p + 2], ZR.at[p], z_s.at[p], z_r.at[p], across)

    def step(k, gradient):
        cols = slice(k * 128, k * 128 + 128)
        velocity = 0.5 * MO[:, cols] + gradient
        o_vel[:, cols] = velocity
        CUR[:, cols] = WT[:, cols] - LEARNING_RATE * velocity

    def transpose_out(p):
        cols = slice(p * 256, p * 256 + 256)
        for i in range(16):
            to = lax.rem(w + i, 16)
            rows = pl.ds(pl.multiple_of(to * 8, 8), 8)
            send(CUR.at[rows, cols], RX.at[w, :, cols], a_s.at[p], a_r.at[p], {"worker": to, "tok": flip})

    def finish(p):
        z[p].wait_recv()
        for k in range(2):
            step(2 * p + k, mine[0, 0, 2 * p + k] + ZR[p, k])
        transpose_out(p)

    w1, w2 = {}, {}

    def across_one():
        for dy in (2, 1, 3, 0):
            zf[dy].wait_recv()
            mine[0, dy, 6:8] = mine[0, dy, 6:8] + ZF[dy]
        for k in range(2):
            w1[k] = send(mine.at[0, 2, 6 + k], W1.at[k], w1_s.at[k], w1_r.at[k], (up, down)[k])

    def across_two():
        for k in range(2):
            dy = (1, 3)[k]
            w1[k].wait_recv()
            mine[0, dy, 6 + k] = mine[0, dy, 6 + k] + W1[k]
        for side in range(2):
            w2[side] = send(
                mine.at[0, (1, 3)[side], 6:8], W2.at[side], w2_s.at[side], w2_r.at[side], (up, down)[side]
            )

    w_load.wait()
    m_load.wait()
    second(0)
    second(1)
    own(0)
    across_one()
    second(2)
    finish(0)
    own(1)
    across_two()
    finish(1)

    def distances(half):
        for bi in range(4):
            for bj in range(bi, 4):
                acc = {}
                for tile in range(4):
                    cols = slice(half * 512 + tile * 128, half * 512 + tile * 128 + 128)
                    left = [RX[4 * bi + i, :, cols] for i in range(4)]
                    right = left if bi == bj else [RX[4 * bj + i, :, cols] for i in range(4)]
                    for i in range(4):
                        for j in range(i + 1 if bi == bj else 0, 4):
                            diff = left[i] - right[j]
                            acc[i, j] = diff * diff if tile == 0 else acc[i, j] + diff * diff
                for (i, j), total in acc.items():
                    row = jnp.sum(total, axis=0, keepdims=True)
                    for a, b in ((4 * bi + i, 4 * bj + j), (4 * bj + j, 4 * bi + i)):
                        at = half * 256 + a * 16 + b
                        DP[at : at + 1, :] = row

    def wait_rows(p):
        wait_bytes(RX.at[:, :, p * 256 : p * 256 + 256], a_r.at[p])

    own(2)
    wait_rows(0)
    wait_rows(1)
    distances(0)
    finish(2)
    for side in range(2):
        w2[side].wait_recv()
    for k in range(2):
        step(6 + k, mine[0, 0, 6 + k] + W2[0, k] + W2[1, k])
    transpose_out(3)

    wait_bytes(MR.at[0:15], m_r.at[0])
    wait_rows(2)
    wait_rows(3)
    distances(1)

    packed = lax.dot_general(
        jnp.ones((8, 128), F32), DP[...], (((1,), (1,)), ((), ())), precision=HIGHEST, preferred_element_type=F32
    )
    PAY[0] = jnp.zeros((8, 128), F32)
    for r in range(4):
        PAY[0, r : r + 1, :] = packed[0:1, r * 128 : r * 128 + 128]
    for stage, (peers, got) in enumerate(((tok_peers, R1), (work_peers, R2))):
        for i, peer in enumerate(peers):
            send(PAY.at[stage, 0:4], got.at[i, 0:4], r_s.at[stage], r_r.at[stage], peer)
        total = PAY[stage, 0:4]
        wait_bytes(got.at[:, 0:4], r_r.at[stage])
        for i in range(15):
            total = total + got[i, 0:4]
        PAY[stage + 1, 0:4] = total

    row = lax.broadcasted_iota(jnp.int32, (32, 128), 0)
    lane = lax.broadcasted_iota(jnp.int32, (32, 128), 1)
    me = row & 15
    base = row - me
    masks = [
        (lane == base + other).astype(F32) for other in (me ^ 1, me ^ 2, (me + 12) & 15, (me + 4) & 15)
    ]
    eye = (lane == row).astype(F32)
    spread = jnp.concatenate([jnp.broadcast_to(PAY[2, r : r + 1, :], (8, 128)) for r in range(4)], axis=0)
    spread = jnp.where((lane >> 4) == (row & 7), spread, 0.0)
    from_lane = lax.broadcasted_iota(jnp.int32, (128, 128), 0)
    to_lane = lax.broadcasted_iota(jnp.int32, (128, 128), 1)
    pick = ((from_lane & 15) == (to_lane & 15)).astype(F32)
    dist2 = jnp.dot(spread, pick, precision=HIGHEST, preferred_element_type=F32)
    dist2 = jnp.where((lane >> 4) == (row >> 4), dist2, 0.0)
    pad = jnp.zeros((96, 128), F32)

    mixing = MR[:, 0, :]
    lane16 = lax.broadcasted_iota(jnp.int32, (16, 128), 1)
    shares = mixing / jnp.sum(mixing, axis=1, keepdims=True)
    share = []
    for k in range(4):
        one = jnp.sum(jnp.where(lane16 == k + 1, shares, 0.0), axis=1, keepdims=True)
        share.append(jnp.concatenate([one, one], axis=0))

    for round_index in range(ROUNDS):
        radius = clip[round_index].astype(F32) * (math.sqrt(D * KV_WIDTH) / 1000.0)
        moves = []
        for k in range(4):
            squares = jnp.sum(dist2 * masks[k], axis=1, keepdims=True)
            factor = radius / jnp.maximum(jnp.sqrt(jnp.maximum(squares, 0.0)), radius)
            moves.append(jnp.broadcast_to(share[k] * factor, (32, 128)))
            KC[round_index, k] = moves[k]
        if round_index == 0:
            mixer = eye * (1.0 - (moves[0] + moves[1] + moves[2] + moves[3]))
            for k in range(4):
                mixer = mixer + masks[k] * moves[k]
            left = jnp.dot(
                mixer, jnp.concatenate([dist2, pad], axis=0), precision=HIGHEST, preferred_element_type=F32
            )
            both = lax.dot_general(
                left, jnp.concatenate([mixer, pad], axis=0), (((1,), (1,)), ((), ())),
                precision=HIGHEST, preferred_element_type=F32,
            )
            diagonal = both * eye
            by_row = jnp.sum(diagonal, axis=1, keepdims=True)
            by_lane = jnp.sum(diagonal, axis=0, keepdims=True)
            dist2 = both - 0.5 * (by_row + by_lane)

    neighbours = [(i ^ 1, i ^ 2, (i - 4) % 16, (i + 4) % 16) for i in range(16)]

    def mixed(round_index, half, blocks):
        out = []
        for i in range(16):
            moved = None
            for k, j in enumerate(neighbours[i]):
                by = jnp.broadcast_to(KC[round_index, k, half * 16 + i : half * 16 + i + 1, :], (8, 128))
                term = by * (blocks[j] - blocks[i])
                moved = term if moved is None else moved + term
            out.append(blocks[i] + moved)
        return out

    here = pl.ds(pl.multiple_of(w * 8, 8), 8)
    for half in range(2):
        for tile in range(4):
            cols = slice(half * 512 + tile * 128, half * 512 + tile * 128 + 128)
            blocks = [RX[i, :, cols] for i in range(16)]
            for round_index in range(ROUNDS):
                blocks = mixed(round_index, half, blocks)
            for i in range(16):
                NEW[i, :, cols] = blocks[i]
        cols = slice(half * 512, half * 512 + 512)
        for i in range(16):
            to = lax.rem(w + i, 16)
            send(NEW.at[to, :, cols], NR.at[here, cols], b_s.at[half], b_r.at[half], {"worker": to, "tok": flip})

    for cp in d + list(y1.values()) + list(y2.values()) + list(z.values()):
        cp.wait_send()
    for cp in list(zf.values()) + list(w1.values()) + list(w2.values()):
        cp.wait_send()
    wait_bytes(MR.at[0:15], m_s.at[0])
    for stage, got in enumerate((R1, R2)):
        wait_bytes(got.at[:, 0:4], r_s.at[stage])
    for p in range(4):
        wait_bytes(CUR.at[:, p * 256 : p * 256 + 256], a_s.at[p])
    for half in range(2):
        cols = slice(half * 512, half * 512 + 512)
        wait_bytes(NR.at[:, cols], b_r.at[half])
        o_new[:, cols] = NR[:, cols]
    for half in range(2):
        wait_bytes(NR.at[:, half * 512 : half * 512 + 512], b_s.at[half])


def per_device(inputs, cotangent, weights, momentum, mix_weights, clip_radius):
    vmem = pl.BlockSpec(memory_space=pltpu.VMEM)
    hbm = pl.BlockSpec(memory_space=pl.ANY)
    dma = pltpu.SemaphoreType.DMA
    block = jax.ShapeDtypeStruct((128, 1024), F32)
    new, velocity = pl.pallas_call(
        kernel,
        out_shape=(block, block),
        in_specs=[hbm, hbm, hbm, hbm, vmem, pl.BlockSpec(memory_space=pltpu.SMEM)],
        out_specs=(vmem, vmem),
        scratch_shapes=[
            pltpu.VMEM((8, 1536, 256), BF16),
            pltpu.VMEM((4, 1536, 256), BF16),
            pltpu.VMEM((2, 2, 4, 8, 128, 128), F32),
            pltpu.VMEM((2, 4, 8, 128, 128), F32),
            pltpu.VMEM((6, 2, 128, 128), F32),
            pltpu.VMEM((2, 6, 2, 128, 128), F32),
            pltpu.VMEM((3, 2, 128, 128), F32),
            pltpu.VMEM((4, 2, 128, 128), F32),
            pltpu.VMEM((2, 128, 128), F32),
            pltpu.VMEM((2, 2, 128, 128), F32),
            pltpu.VMEM((128, 1024), F32),
            pltpu.VMEM((128, 1024), F32),
            pltpu.VMEM((128, 1024), F32),
            pltpu.VMEM((16, 8, 1024), F32),
            pltpu.VMEM((16, 8, 1024), F32),
            pltpu.VMEM((128, 1024), F32),
            pltpu.VMEM((512, 128), F32),
            pltpu.VMEM((3, 8, 128), F32),
            pltpu.VMEM((15, 8, 128), F32),
            pltpu.VMEM((15, 8, 128), F32),
            pltpu.VMEM((8, 128), F32),
            pltpu.VMEM((16, 8, 128), F32),
            pltpu.VMEM((2, 4, 32, 128), F32),
            dma((14,)),
            dma((8,)), dma((8,)),
            dma((6,)), dma((6,)),
            dma((2, 6)), dma((2, 6)),
            dma((3,)), dma((3,)),
            dma((4,)), dma((4,)),
            dma((2,)), dma((2,)),
            dma((2,)), dma((2,)),
            dma((4,)), dma((4,)),
            dma((1,)), dma((1,)),
            dma((2,)), dma((2,)),
            dma((2,)), dma((2,)),
        ],
        compiler_params=pltpu.CompilerParams(
            collective_id=0, has_side_effects=True, vmem_limit_bytes=56 * 1024 * 1024
        ),
    )(inputs[0], cotangent[0], weights[0], momentum[0], mix_weights, clip_radius)
    return (new[None], velocity[None])


def solution(mesh):
    placed = (
        P("worker", "tok", None),
        P("worker", "tok", None),
        P("worker", "tok", None),
        P("worker", "tok", None),
        P("worker", None),
        P(),
    )
    return jax.shard_map(
        per_device,
        mesh=mesh,
        in_specs=placed,
        out_specs=(P("worker", "tok", None), P("worker", "tok", None)),
        check_vma=False,
    )
```

```python
import math

import jax
import jax.numpy as jnp
from jax import lax
from jax.experimental import pallas as pl
from jax.experimental.pallas import tpu as pltpu
from jax.sharding import PartitionSpec as P

D = 2048
KV_WIDTH = 512
ROUNDS = 2
LEARNING_RATE = 0.25

MESH = pl.DeviceIdType.MESH
F32 = jnp.float32
BF16 = jnp.bfloat16
HIGHEST = lax.Precision.HIGHEST

ORDER = ((1, 2), (0, 2), (1, 1), (0, 1), (1, 3), (0, 3), (1, 0), (0, 0))
PAIRS = 3


def kernel(
    feat, cot, wts, mom, mix, clip, o_move, o_grad,
    F, C, PA, PR, Y1, Y2, ZR, ZF, W1, W2, WT, MO, CUR, GR, RX, NEW, DP, PAY, R1, R2, MS, MR, KC,
    ld, d_s, d_r, y1_s, y1_r, y2_s, y2_r, z_s, z_r, zf_s, zf_r, w1_s, w1_r, w2_s, w2_r,
    a_s, a_r, m_s, m_r, r_s, r_r, b_s, b_r, g_s, far,
):
    t = lax.axis_index("tok")
    w = lax.axis_index("worker")
    q, y, c = t // 8, (t // 2) % 4, t % 2
    flip = (1 - q) * 8 + y * 2 + c
    sibling = {"worker": w, "tok": q * 8 + y * 2 + (1 - c)}
    up = {"worker": w, "tok": q * 8 + lax.rem(y + 1, 4) * 2 + c}
    down = {"worker": w, "tok": q * 8 + lax.rem(y + 3, 4) * 2 + c}
    across = {"worker": w, "tok": flip}
    h, x = w // 4, w % 4
    tok_peers = [
        {"worker": w, "tok": (q + dq) % 2 * 8 + lax.rem(y + dy, 4) * 2 + (c + dc) % 2}
        for dy in (2, 1, 3, 0) for dq in (1, 0) for dc in (1, 0)
    ][:-1]
    others = [lax.rem(h + dh, 4) * 4 + lax.rem(x + dx, 4) for dx in (2, 1, 3, 0) for dh in (2, 1, 3, 0)]
    work_peers = [{"worker": other, "tok": flip} for other in others[:-1]]
    beyond = lax.rem(h + 2 * q + 3, 4)
    next_to = [sibling, up, down, across] + [
        {"worker": h * 4 + lax.rem(x + 1, 4), "tok": t},
        {"worker": h * 4 + lax.rem(x + 3, 4), "tok": t},
        {"worker": beyond * 4 + x, "tok": flip},
    ]

    def tell(n):
        for peer in next_to:
            pl.semaphore_signal(far.at[n], inc=1, device_id=peer, device_id_type=MESH)

    def heard(n):
        pl.semaphore_wait(far.at[n], 7)

    barrier = pltpu.get_barrier_semaphore()

    def load(src, dst, i):
        cp = pltpu.make_async_copy(src, dst, ld.at[i])
        cp.start()
        return cp

    def send(src, dst, ss, rs, peer):
        cp = pltpu.make_async_remote_copy(
            src_ref=src, dst_ref=dst, send_sem=ss, recv_sem=rs, device_id=peer, device_id_type=MESH
        )
        cp.start()
        return cp

    def wait_bytes(ref, sem):
        pltpu.make_async_copy(ref, ref, sem).wait()

    def feat_block(j):
        dq, dy = ORDER[j]
        chip = (q + dq) % 2 * 4 + lax.rem(y + dy, 4)
        return feat.at[:, pl.ds(pl.multiple_of(chip * 256, 256), 256)]

    def load_feat(j):
        f_loads[j] = load(feat_block(j), F.at[j], j)

    def load_cot(n):
        c_loads[n] = load(cot.at[:, n * 256 : (n + 1) * 256], C.at[n], 8 + n)

    f_loads, c_loads = {}, {}
    load_feat(0)
    load_cot(0)
    load_feat(1)
    for peer in next_to:
        pl.semaphore_signal(barrier, inc=1, device_id=peer, device_id_type=MESH)

    MS[...] = jnp.zeros_like(MS)
    MS[0:1, 0:5] = mix[...].astype(F32)
    MR[w] = MS[...]
    for half in range(2):
        for i in range(16):
            DP[half * 256 + i * 17 : half * 256 + i * 17 + 1, :] = jnp.zeros((1, 128), F32)

    mine = PA.at[c]

    def product(j, n):
        dq, dy = ORDER[j]
        r = lax.dot_general(F[j], C[n], (((0,), (0,)), ((), ())), preferred_element_type=F32)
        for core in range(2):
            for k in range(2):
                PA[core, dq, dy, 2 * n + k] = r[core * 128 : core * 128 + 128, k * 128 : k * 128 + 128]

    d, zf, y1 = {}, {}, {}

    def first_across(dy):
        zf[dy] = send(mine.at[1, dy, 6:8], ZF.at[dy], zf_s.at[dy], zf_r.at[dy], across)

    def opposite(n):
        d[n].wait_recv()
        for dq in range(2):
            for k in (2 * n, 2 * n + 1):
                mine[dq, 2, k] = mine[dq, 2, k] + PR[dq, 2, k]
        if n < PAIRS:
            for k in (2 * n, 2 * n + 1):
                y1[k] = send(mine.at[:, 2, k], Y1.at[k], y1_s.at[k], y1_r.at[k], (up, down)[k % 2])
        else:
            first_across(2)

    for n in range(4):
        for j in range(2):
            if n == 0:
                f_loads[j].wait()
            if j == 0:
                c_loads[n].wait()
            if n == 0 and j == 0:
                load_cot(1)
                load_cot(2)
            product(j, n)
        if n == 0:
            load_cot(3)
            load_feat(2)
            pl.semaphore_wait(barrier, 7)
        else:
            load_feat(2 * n + 1)
            if n < 3:
                load_feat(2 * n + 2)
        d[n] = send(PA.at[1 - c, :, 2, 2 * n : 2 * n + 2], PR.at[:, 2, 2 * n : 2 * n + 2], d_s.at[n], d_r.at[n], sibling)
        if n >= 1:
            opposite(n - 1)
    w_load, m_load = load(wts, WT, 12), load(mom, MO, 13)
    tell(0)

    def add_sibling(j):
        dq, dy = ORDER[j]
        d[j + 2].wait_recv()
        mine[dq, dy] = mine[dq, dy] + PR[dq, dy]
        if dq == 1:
            first_across(dy)

    y2 = {}

    def along(side, k):
        to, dy = ((up, 1), (down, 3))[side]
        y2[side, k] = send(mine.at[:, dy, k], Y2.at[side, k], y2_s.at[side, k], y2_r.at[side, k], to)

    def plain(k):
        along(1 - k % 2, k)

    def joined(k):
        side, dy = k % 2, (1, 3)[k % 2]
        y1[k].wait_recv()
        mine[:, dy, k] = mine[:, dy, k] + Y1[k]
        along(side, k)

    for j in range(2, 8):
        dq, dy = ORDER[j]
        f_loads[j].wait()
        for n in range(4):
            product(j, n)
        d[j + 2] = send(PA.at[1 - c, dq, dy], PR.at[dq, dy], d_s.at[j + 2], d_r.at[j + 2], sibling)
        if j == 2:
            opposite(3)
        else:
            add_sibling(j - 1)
        if j == 4:
            plain(1)
            heard(0)
            tell(1)
        if j == 6:
            plain(0)
            heard(1)
            tell(2)

    z = {}

    def own(k):
        y2[0, k].wait_recv()
        y2[1, k].wait_recv()
        mine[:, 0, k] = mine[:, 0, k] + Y2[0, k] + Y2[1, k]
        z[k] = send(mine.at[1, 0, k], ZR.at[k], z_s.at[k], z_r.at[k], across)

    def step(k, gradient):
        cols = slice(k * 128, k * 128 + 128)
        velocity = 0.5 * MO[:, cols] + gradient
        GR[:, cols] = gradient
        CUR[:, cols] = WT[:, cols] - LEARNING_RATE * velocity

    def transpose_out(k):
        cols = slice(k * 128, k * 128 + 128)
        for to in others:
            rows = pl.ds(pl.multiple_of(to * 8, 8), 8)
            send(CUR.at[rows, cols], RX.at[w, :, cols], a_s.at[k], a_r.at[k], {"worker": to, "tok": flip})

    def finish(k):
        z[k].wait_recv()
        step(k, mine[0, 0, k] + ZR[k])
        transpose_out(k)

    w1, w2 = {}, {}

    def across_one():
        for dy in (2, 1, 3, 0):
            zf[dy].wait_recv()
            mine[0, dy, 6:8] = mine[0, dy, 6:8] + ZF[dy]
        for k in range(2):
            w1[k] = send(mine.at[0, 2, 6 + k], W1.at[k], w1_s.at[k], w1_r.at[k], (up, down)[k])

    def across_two(k):
        dy = (1, 3)[k]
        w1[k].wait_recv()
        mine[0, dy, 6 + k] = mine[0, dy, 6 + k] + W1[k]
        for side in range(2):
            w2[side, k] = send(
                mine.at[0, (1, 3)[side], 6 + k], W2.at[side, k], w2_s.at[side, k], w2_r.at[side, k], (up, down)[side]
            )

    def finish_across(k):
        for side in range(2):
            w2[side, k].wait_recv()
        step(6 + k, mine[0, 0, 6 + k] + W2[0, k] + W2[1, k])
        transpose_out(6 + k)

    joined(0)
    joined(1)
    add_sibling(7)
    heard(2)
    tell(3)
    joined(2)
    plain(2)
    plain(3)
    joined(3)
    w_load.wait()
    m_load.wait()
    heard(3)
    for peer in work_peers:
        send(MS, MR.at[w], m_s.at[0], m_r.at[0], peer)
    own(0)
    own(1)
    across_one()
    joined(4)
    plain(4)
    plain(5)
    joined(5)
    finish(0)
    finish(1)
    own(2)
    own(3)
    across_two(0)
    across_two(1)
    finish(2)
    finish(3)

    def distances(half):
        for bi in range(4):
            for bj in range(bi, 4):
                which = [(i, j) for i in range(4) for j in range(i + 1 if bi == bj else 0, 4)]

                def tiles(tile, acc, bi=bi, bj=bj, which=which):
                    cols = pl.ds(pl.multiple_of(half * 512 + tile * 128, 128), 128)
                    left = [RX[4 * bi + i, :, cols] for i in range(4)]
                    right = left if bi == bj else [RX[4 * bj + i, :, cols] for i in range(4)]
                    diffs = [left[i] - right[j] for i, j in which]
                    return tuple(a + e * e for a, e in zip(acc, diffs))

                acc = lax.fori_loop(0, 4, tiles, tuple(jnp.zeros((8, 128), F32) for _ in which))
                for (i, j), total in zip(which, acc):
                    row = jnp.sum(total, axis=0, keepdims=True)
                    for a, b in ((4 * bi + i, 4 * bj + j), (4 * bj + j, 4 * bi + i)):
                        at = half * 256 + a * 16 + b
                        DP[at : at + 1, :] = row

    def wait_rows(half):
        for k in range(4 * half, 4 * half + 4):
            wait_bytes(RX.at[:, :, k * 128 : k * 128 + 128], a_r.at[k])

    own(4)
    own(5)
    finish(4)
    finish(5)
    finish_across(0)
    finish_across(1)
    put = pltpu.make_async_copy(GR, o_grad, g_s.at[0])
    put.start()
    wait_rows(0)
    distances(0)
    wait_bytes(MR.at[0:15], m_r.at[0])
    wait_rows(1)
    distances(1)

    packed = lax.dot_general(
        jnp.ones((8, 128), F32), DP[...], (((1,), (1,)), ((), ())), precision=HIGHEST, preferred_element_type=F32
    )
    PAY[0] = jnp.zeros((8, 128), F32)
    for r in range(4):
        PAY[0, r : r + 1, :] = packed[0:1, r * 128 : r * 128 + 128]
    for stage, (peers, got) in enumerate(((tok_peers, R1), (work_peers, R2))):
        for i, peer in enumerate(peers):
            send(PAY.at[stage, 0:4], got.at[i, 0:4], r_s.at[stage], r_r.at[stage], peer)
        total = PAY[stage, 0:4]
        wait_bytes(got.at[:, 0:4], r_r.at[stage])
        for i in range(15):
            total = total + got[i, 0:4]
        PAY[stage + 1, 0:4] = total

    row = lax.broadcasted_iota(jnp.int32, (32, 128), 0)
    lane = lax.broadcasted_iota(jnp.int32, (32, 128), 1)
    me = row & 15
    base = row - me
    masks = [
        (lane == base + other).astype(F32) for other in (me ^ 1, me ^ 2, (me + 12) & 15, (me + 4) & 15)
    ]
    eye = (lane == row).astype(F32)
    spread = jnp.concatenate([jnp.broadcast_to(PAY[2, r : r + 1, :], (8, 128)) for r in range(4)], axis=0)
    spread = jnp.where((lane >> 4) == (row & 7), spread, 0.0)
    from_lane = lax.broadcasted_iota(jnp.int32, (128, 128), 0)
    to_lane = lax.broadcasted_iota(jnp.int32, (128, 128), 1)
    pick = ((from_lane & 15) == (to_lane & 15)).astype(F32)
    dist2 = jnp.dot(spread, pick, precision=HIGHEST, preferred_element_type=F32)
    dist2 = jnp.where((lane >> 4) == (row >> 4), dist2, 0.0)
    pad = jnp.zeros((96, 128), F32)

    mixing = MR[:, 0, :]
    lane16 = lax.broadcasted_iota(jnp.int32, (16, 128), 1)
    shares = mixing / jnp.sum(mixing, axis=1, keepdims=True)
    share = []
    for k in range(4):
        one = jnp.sum(jnp.where(lane16 == k + 1, shares, 0.0), axis=1, keepdims=True)
        share.append(jnp.concatenate([one, one], axis=0))

    for round_index in range(ROUNDS):
        radius = clip[round_index].astype(F32) * (math.sqrt(D * KV_WIDTH) / 1000.0)
        moves = []
        for k in range(4):
            squares = jnp.sum(dist2 * masks[k], axis=1, keepdims=True)
            factor = radius / jnp.maximum(jnp.sqrt(jnp.maximum(squares, 0.0)), radius)
            moves.append(jnp.broadcast_to(share[k] * factor, (32, 128)))
            KC[round_index, k] = moves[k]
        if round_index == 0:
            mixer = eye * (1.0 - (moves[0] + moves[1] + moves[2] + moves[3]))
            for k in range(4):
                mixer = mixer + masks[k] * moves[k]
            left = jnp.dot(
                mixer, jnp.concatenate([dist2, pad], axis=0), precision=HIGHEST, preferred_element_type=F32
            )
            both = lax.dot_general(
                left, jnp.concatenate([mixer, pad], axis=0), (((1,), (1,)), ((), ())),
                precision=HIGHEST, preferred_element_type=F32,
            )
            diagonal = both * eye
            by_row = jnp.sum(diagonal, axis=1, keepdims=True)
            by_lane = jnp.sum(diagonal, axis=0, keepdims=True)
            dist2 = both - 0.5 * (by_row + by_lane)

    neighbours = [(i ^ 1, i ^ 2, (i - 4) % 16, (i + 4) % 16) for i in range(16)]

    def mixed(round_index, half, blocks):
        out = []
        for i in range(16):
            moved = None
            for k, j in enumerate(neighbours[i]):
                by = jnp.broadcast_to(KC[round_index, k, half * 16 + i : half * 16 + i + 1, :], (8, 128))
                term = by * (blocks[j] - blocks[i])
                moved = term if moved is None else moved + term
            out.append(moved)
        return out

    here = pl.ds(pl.multiple_of(w * 8, 8), 8)
    for half in range(2):

        def columns(tile, _, half=half):
            cols = pl.ds(pl.multiple_of(half * 512 + tile * 128, 128), 128)
            blocks = [RX[i, :, cols] for i in range(16)]
            first = mixed(0, half, blocks)
            second = mixed(1, half, [b + m for b, m in zip(blocks, first)])
            for i in range(16):
                NEW[i, :, cols] = first[i] + second[i]
            return 0

        lax.fori_loop(0, 4, columns, 0)
        cols = slice(half * 512, half * 512 + 512)
        for to in others:
            send(NEW.at[to, :, cols], o_move.at[here, cols], b_s.at[half], b_r.at[half], {"worker": to, "tok": flip})

    for cp in list(d.values()) + list(y1.values()) + list(y2.values()) + list(z.values()):
        cp.wait_send()
    for cp in list(zf.values()) + list(w1.values()) + list(w2.values()):
        cp.wait_send()
    wait_bytes(MR.at[0:15], m_s.at[0])
    for stage, got in enumerate((R1, R2)):
        wait_bytes(got.at[:, 0:4], r_s.at[stage])
    for k in range(8):
        wait_bytes(CUR.at[:, k * 128 : k * 128 + 128], a_s.at[k])
    put.wait()
    for half in range(2):
        cols = slice(half * 512, half * 512 + 512)
        wait_bytes(NEW.at[:, :, cols], b_s.at[half])
        wait_bytes(o_move.at[:, cols], b_r.at[half])


def per_device(inputs, cotangent, weights, momentum, mix_weights, clip_radius):
    vmem = pl.BlockSpec(memory_space=pltpu.VMEM)
    hbm = pl.BlockSpec(memory_space=pl.ANY)
    dma = pltpu.SemaphoreType.DMA
    block = jax.ShapeDtypeStruct((128, 1024), F32)
    moved, gradient = pl.pallas_call(
        kernel,
        out_shape=(block, block),
        in_specs=[hbm, hbm, hbm, hbm, vmem, pl.BlockSpec(memory_space=pltpu.SMEM)],
        out_specs=(hbm, hbm),
        scratch_shapes=[
            pltpu.VMEM((8, 1536, 256), BF16),
            pltpu.VMEM((4, 1536, 256), BF16),
            pltpu.VMEM((2, 2, 4, 8, 128, 128), F32),
            pltpu.VMEM((2, 4, 8, 128, 128), F32),
            pltpu.VMEM((6, 2, 128, 128), F32),
            pltpu.VMEM((2, 6, 2, 128, 128), F32),
            pltpu.VMEM((6, 128, 128), F32),
            pltpu.VMEM((4, 2, 128, 128), F32),
            pltpu.VMEM((2, 128, 128), F32),
            pltpu.VMEM((2, 2, 128, 128), F32),
            pltpu.VMEM((128, 1024), F32),
            pltpu.VMEM((128, 1024), F32),
            pltpu.VMEM((128, 1024), F32),
            pltpu.VMEM((128, 1024), F32),
            pltpu.VMEM((16, 8, 1024), F32),
            pltpu.VMEM((16, 8, 1024), F32),
            pltpu.VMEM((512, 128), F32),
            pltpu.VMEM((3, 8, 128), F32),
            pltpu.VMEM((15, 8, 128), F32),
            pltpu.VMEM((15, 8, 128), F32),
            pltpu.VMEM((8, 128), F32),
            pltpu.VMEM((16, 8, 128), F32),
            pltpu.VMEM((2, 4, 32, 128), F32),
            dma((14,)),
            dma((10,)), dma((10,)),
            dma((6,)), dma((6,)),
            dma((2, 6)), dma((2, 6)),
            dma((6,)), dma((6,)),
            dma((4,)), dma((4,)),
            dma((2,)), dma((2,)),
            dma((2, 2)), dma((2, 2)),
            dma((8,)), dma((8,)),
            dma((1,)), dma((1,)),
            dma((2,)), dma((2,)),
            dma((2,)), dma((2,)),
            dma((1,)),
            pltpu.SemaphoreType.REGULAR((4,)),
        ],
        compiler_params=pltpu.CompilerParams(
            collective_id=0, has_side_effects=True, vmem_limit_bytes=56 * 1024 * 1024
        ),
    )(inputs[0], cotangent[0], weights[0], momentum[0], mix_weights, clip_radius)
    velocity = 0.5 * momentum[0] + gradient
    new = (weights[0] - LEARNING_RATE * velocity) + moved
    return (new[None], velocity[None])


def solution(mesh):
    placed = (
        P("worker", "tok", None),
        P("worker", "tok", None),
        P("worker", "tok", None),
        P("worker", "tok", None),
        P("worker", None),
        P(),
    )
    return jax.shard_map(
        per_device,
        mesh=mesh,
        in_specs=placed,
        out_specs=(P("worker", "tok", None), P("worker", "tok", None)),
        check_vma=False,
    )
```

```python
import math

import jax
import jax.numpy as jnp
from jax import lax
from jax.experimental import pallas as pl
from jax.experimental.pallas import tpu as pltpu
from jax.sharding import PartitionSpec as P

D = 2048
KV_WIDTH = 512
ROUNDS = 2
LEARNING_RATE = 0.25

MESH = pl.DeviceIdType.MESH
F32 = jnp.float32
BF16 = jnp.bfloat16
HIGHEST = lax.Precision.HIGHEST

ORDER = ((1, 2), (0, 2), (1, 1), (0, 1), (1, 3), (0, 3), (1, 0), (0, 0))
PAIRS = 3


def kernel(
    feat, cot, wts, mom, mix, clip, o_move, o_grad,
    F, C, PA, PR, Y1, Y2, ZR, ZF, W1, W2, WT, MO, CUR, GR, RX, NEW, DP, PAY, R1, R2, MS, MR, KC,
    ld, d_s, d_r, y1_s, y1_r, y2_s, y2_r, z_s, z_r, zf_s, zf_r, w1_s, w1_r, w2_s, w2_r,
    a_s, a_r, m_s, m_r, r_s, r_r, b_s, b_r, g_s, far,
):
    t = lax.axis_index("tok")
    w = lax.axis_index("worker")
    q, y, c = lax.div(t, 8), lax.rem(lax.div(t, 2), 4), lax.rem(t, 2)

    def load(src, dst, i):
        cp = pltpu.make_async_copy(src, dst, ld.at[i])
        cp.start()
        return cp

    def feat_block(j):
        dq, dy = ORDER[j]
        chip = (1 - q if dq else q) * 4 + lax.rem(y + dy, 4)
        return feat.at[:, pl.ds(pl.multiple_of(chip * 256, 256), 256)]

    def load_feat(j):
        f_loads[j] = load(feat_block(j), F.at[j], j)

    def load_cot(n):
        c_loads[n] = load(cot.at[:, n * 256 : (n + 1) * 256], C.at[n], 8 + n)

    f_loads, c_loads = {}, {}
    load_feat(0)
    load_cot(0)
    load_feat(1)

    def chip_at(z, y, c):
        return z * 8 + y * 2 + c

    h, x = lax.div(w, 4), lax.rem(w, 4)
    ys = [y] + [lax.rem(y + i, 4) for i in range(1, 4)]
    hs = [h] + [lax.rem(h + i, 4) for i in range(1, 4)]
    xs = [x] + [lax.rem(x + i, 4) for i in range(1, 4)]
    flip = chip_at(1 - q, y, c)
    sibling = {"worker": w, "tok": chip_at(q, y, 1 - c)}
    up = {"worker": w, "tok": chip_at(q, ys[1], c)}
    down = {"worker": w, "tok": chip_at(q, ys[3], c)}
    across = {"worker": w, "tok": flip}
    beyond = lax.rem(h + 2 * q + 3, 4)
    next_to = [sibling, up, down, across] + [
        {"worker": h * 4 + xs[1], "tok": t},
        {"worker": h * 4 + xs[3], "tok": t},
        {"worker": beyond * 4 + x, "tok": flip},
    ]
    barrier = pltpu.get_barrier_semaphore()
    for peer in next_to:
        pl.semaphore_signal(barrier, inc=1, device_id=peer, device_id_type=MESH)

    def tell(n):
        for peer in next_to:
            pl.semaphore_signal(far.at[n], inc=1, device_id=peer, device_id_type=MESH)

    def heard(n):
        pl.semaphore_wait(far.at[n], 7)

    def send(src, dst, ss, rs, peer):
        cp = pltpu.make_async_remote_copy(
            src_ref=src, dst_ref=dst, send_sem=ss, recv_sem=rs, device_id=peer, device_id_type=MESH
        )
        cp.start()
        return cp

    def wait_bytes(ref, sem):
        pltpu.make_async_copy(ref, ref, sem).wait()

    mine = PA.at[c]

    def product(j, n):
        dq, dy = ORDER[j]
        r = lax.dot_general(F[j], C[n], (((0,), (0,)), ((), ())), preferred_element_type=F32)
        for core in range(2):
            for k in range(2):
                PA[core, dq, dy, 2 * n + k] = r[core * 128 : core * 128 + 128, k * 128 : k * 128 + 128]

    d, zf, y1 = {}, {}, {}

    def first_across(dy):
        zf[dy] = send(mine.at[1, dy, 6:8], ZF.at[dy], zf_s.at[dy], zf_r.at[dy], across)

    def opposite(n):
        d[n].wait_recv()
        for dq in range(2):
            for k in (2 * n, 2 * n + 1):
                mine[dq, 2, k] = mine[dq, 2, k] + PR[dq, 2, k]
        if n < PAIRS:
            for k in (2 * n, 2 * n + 1):
                y1[k] = send(mine.at[:, 2, k], Y1.at[k], y1_s.at[k], y1_r.at[k], (up, down)[k % 2])
        else:
            first_across(2)

    for n in range(4):
        for j in range(2):
            if n == 0 and j == 0:
                load_cot(1)
            if n == 0:
                f_loads[j].wait()
            if j == 0:
                c_loads[n].wait()
            if n == 0 and j == 0:
                load_cot(2)
            product(j, n)
        if n == 0:
            load_cot(3)
            load_feat(2)
            pl.semaphore_wait(barrier, 7)
        else:
            load_feat(2 * n + 1)
            if n < 3:
                load_feat(2 * n + 2)
        d[n] = send(PA.at[1 - c, :, 2, 2 * n : 2 * n + 2], PR.at[:, 2, 2 * n : 2 * n + 2], d_s.at[n], d_r.at[n], sibling)
        if n >= 1:
            opposite(n - 1)
    w_load, m_load = load(wts, WT, 12), load(mom, MO, 13)
    tell(0)
    tok_peers = [
        {"worker": w, "tok": chip_at(z_at, ys[dy], core)}
        for dy in (2, 1, 3, 0) for z_at in (1 - q, q) for core in (1 - c, c)
    ][:-1]
    others = [hs[dh] * 4 + xs[dx] for dx in (2, 1, 3, 0) for dh in (2, 1, 3, 0)]
    work_peers = [{"worker": other, "tok": flip} for other in others[:-1]]

    def add_sibling(j):
        dq, dy = ORDER[j]
        d[j + 2].wait_recv()
        mine[dq, dy] = mine[dq, dy] + PR[dq, dy]
        if dq == 1:
            first_across(dy)

    y2 = {}

    def along(side, k):
        to, dy = ((up, 1), (down, 3))[side]
        y2[side, k] = send(mine.at[:, dy, k], Y2.at[side, k], y2_s.at[side, k], y2_r.at[side, k], to)

    def plain(k):
        along(1 - k % 2, k)

    def joined(k):
        side, dy = k % 2, (1, 3)[k % 2]
        y1[k].wait_recv()
        mine[:, dy, k] = mine[:, dy, k] + Y1[k]
        along(side, k)

    for j in range(2, 8):
        dq, dy = ORDER[j]
        f_loads[j].wait()
        for n in range(4):
            product(j, n)
        d[j + 2] = send(PA.at[1 - c, dq, dy], PR.at[dq, dy], d_s.at[j + 2], d_r.at[j + 2], sibling)
        if j == 2:
            opposite(3)
        else:
            add_sibling(j - 1)
        if j == 4:
            plain(1)
            heard(0)
            tell(1)
        if j == 6:
            plain(0)
            heard(1)
            tell(2)

    z = {}

    def own(k):
        y2[0, k].wait_recv()
        y2[1, k].wait_recv()
        mine[:, 0, k] = mine[:, 0, k] + Y2[0, k] + Y2[1, k]
        z[k] = send(mine.at[1, 0, k], ZR.at[k], z_s.at[k], z_r.at[k], across)

    def step(k, gradient):
        cols = slice(k * 128, k * 128 + 128)
        velocity = 0.5 * MO[:, cols] + gradient
        GR[:, cols] = gradient
        CUR[:, cols] = WT[:, cols] - LEARNING_RATE * velocity

    def transpose_out(k):
        cols = slice(k * 128, k * 128 + 128)
        for to in others:
            rows = pl.ds(pl.multiple_of(to * 8, 8), 8)
            send(CUR.at[rows, cols], RX.at[w, :, cols], a_s.at[k], a_r.at[k], {"worker": to, "tok": flip})

    def finish(k):
        z[k].wait_recv()
        step(k, mine[0, 0, k] + ZR[k])
        transpose_out(k)

    w1, w2 = {}, {}

    def across_one():
        for dy in (2, 1, 3, 0):
            zf[dy].wait_recv()
            mine[0, dy, 6:8] = mine[0, dy, 6:8] + ZF[dy]
        for k in range(2):
            w1[k] = send(mine.at[0, 2, 6 + k], W1.at[k], w1_s.at[k], w1_r.at[k], (up, down)[k])

    def across_two(k):
        dy = (1, 3)[k]
        w1[k].wait_recv()
        mine[0, dy, 6 + k] = mine[0, dy, 6 + k] + W1[k]
        for side in range(2):
            w2[side, k] = send(
                mine.at[0, (1, 3)[side], 6 + k], W2.at[side, k], w2_s.at[side, k], w2_r.at[side, k], (up, down)[side]
            )

    def finish_across(k):
        for side in range(2):
            w2[side, k].wait_recv()
        step(6 + k, mine[0, 0, 6 + k] + W2[0, k] + W2[1, k])
        transpose_out(6 + k)

    joined(0)
    joined(1)
    add_sibling(7)
    heard(2)
    tell(3)
    joined(2)
    plain(2)
    plain(3)
    joined(3)
    w_load.wait()
    m_load.wait()
    MS[...] = jnp.zeros_like(MS)
    MS[0:1, 0:5] = mix[...].astype(F32)
    MR[w] = MS[...]
    for half in range(2):
        for i in range(16):
            DP[half * 256 + i * 17 : half * 256 + i * 17 + 1, :] = jnp.zeros((1, 128), F32)
    heard(3)
    for peer in work_peers:
        send(MS, MR.at[w], m_s.at[0], m_r.at[0], peer)
    own(0)
    own(1)
    across_one()
    joined(4)
    plain(4)
    plain(5)
    joined(5)
    finish(0)
    finish(1)
    own(2)
    own(3)
    across_two(0)
    across_two(1)
    finish(2)
    finish(3)

    def distances(half):
        for bi in range(4):
            for bj in range(bi, 4):
                which = [(i, j) for i in range(4) for j in range(i + 1 if bi == bj else 0, 4)]

                def tiles(tile, acc, bi=bi, bj=bj, which=which):
                    cols = pl.ds(pl.multiple_of(half * 512 + tile * 128, 128), 128)
                    left = [RX[4 * bi + i, :, cols] for i in range(4)]
                    right = left if bi == bj else [RX[4 * bj + i, :, cols] for i in range(4)]
                    diffs = [left[i] - right[j] for i, j in which]
                    return tuple(a + e * e for a, e in zip(acc, diffs))

                acc = lax.fori_loop(0, 4, tiles, tuple(jnp.zeros((8, 128), F32) for _ in which))
                for (i, j), total in zip(which, acc):
                    row = jnp.sum(total, axis=0, keepdims=True)
                    for a, b in ((4 * bi + i, 4 * bj + j), (4 * bj + j, 4 * bi + i)):
                        at = half * 256 + a * 16 + b
                        DP[at : at + 1, :] = row

    def wait_rows(half):
        for k in range(4 * half, 4 * half + 4):
            wait_bytes(RX.at[:, :, k * 128 : k * 128 + 128], a_r.at[k])

    def pack(half):
        packed = lax.dot_general(
            jnp.ones((8, 128), F32), DP[half * 256 : half * 256 + 256, :], (((1,), (1,)), ((), ())),
            precision=HIGHEST, preferred_element_type=F32,
        )
        for r in range(2):
            PAY[half, 0, r : r + 1, :] = packed[0:1, r * 128 : r * 128 + 128]

    stages = ((tok_peers, R1), (work_peers, R2))

    def share_out(half, stage):
        peers, got = stages[stage]
        for i, peer in enumerate(peers):
            send(PAY.at[half, stage, 0:2], got.at[half, i, 0:2], r_s.at[half, stage], r_r.at[half, stage], peer)

    def add_up(half, stage):
        got = stages[stage][1]
        wait_bytes(got.at[half, :, 0:2], r_r.at[half, stage])
        parts = [PAY[half, stage, 0:2]] + [got[half, i, 0:2] for i in range(15)]
        while len(parts) > 1:
            parts = [a + b for a, b in zip(parts[::2], parts[1::2])]
        PAY[half, stage + 1, 0:2] = parts[0]

    def constants():
        row = lax.broadcasted_iota(jnp.int32, (16, 128), 0)
        lane = lax.broadcasted_iota(jnp.int32, (16, 128), 1)
        masks = [(lane == other).astype(F32) for other in (row ^ 1, row ^ 2, (row + 12) & 15, (row + 4) & 15)]
        from_lane = lax.broadcasted_iota(jnp.int32, (128, 128), 0)
        to_lane = lax.broadcasted_iota(jnp.int32, (128, 128), 1)
        pick = ((from_lane & 15) == to_lane).astype(F32)
        mixing = MR[:, 0, :]
        shares = mixing / jnp.sum(mixing, axis=1, keepdims=True)
        share = [jnp.sum(jnp.where(lane == k + 1, shares, 0.0), axis=1, keepdims=True) for k in range(4)]
        return (lane >> 4) == (row & 7), masks, (lane == row).astype(F32), pick, share

    def solve(half):
        place, masks, eye, pick, share = constants()
        spread = jnp.concatenate([jnp.broadcast_to(PAY[half, 2, r : r + 1, :], (8, 128)) for r in range(2)], axis=0)
        dist2 = jnp.dot(jnp.where(place, spread, 0.0), pick, precision=HIGHEST, preferred_element_type=F32)
        pad = jnp.zeros((112, 128), F32)
        for round_index in range(ROUNDS):
            radius = clip[round_index].astype(F32) * (math.sqrt(D * KV_WIDTH) / 1000.0)
            moves = []
            for k in range(4):
                squares = jnp.sum(dist2 * masks[k], axis=1, keepdims=True)
                factor = radius / jnp.maximum(jnp.sqrt(jnp.maximum(squares, 0.0)), radius)
                moves.append(jnp.broadcast_to(share[k] * factor, (16, 128)))
                KC[round_index, k, half * 16 : half * 16 + 16, :] = moves[k]
            if round_index == 0:
                mixer = eye * (1.0 - (moves[0] + moves[1] + moves[2] + moves[3]))
                for k in range(4):
                    mixer = mixer + masks[k] * moves[k]
                left = jnp.dot(
                    mixer, jnp.concatenate([dist2, pad], axis=0), precision=HIGHEST, preferred_element_type=F32
                )
                both = lax.dot_general(
                    left, jnp.concatenate([mixer, pad], axis=0), (((1,), (1,)), ((), ())),
                    precision=HIGHEST, preferred_element_type=F32,
                )
                diagonal = both * eye
                by_row = jnp.sum(diagonal, axis=1, keepdims=True)
                by_lane = jnp.sum(diagonal, axis=0, keepdims=True)
                dist2 = both - 0.5 * (by_row + by_lane)

    neighbours = [(i ^ 1, i ^ 2, (i - 4) % 16, (i + 4) % 16) for i in range(16)]

    def mixed(round_index, half, blocks):
        out = []
        for i in range(16):
            moved = None
            for k, j in enumerate(neighbours[i]):
                by = jnp.broadcast_to(KC[round_index, k, half * 16 + i : half * 16 + i + 1, :], (8, 128))
                term = by * (blocks[j] - blocks[i])
                moved = term if moved is None else moved + term
            out.append(moved)
        return out

    here = pl.ds(pl.multiple_of(w * 8, 8), 8)

    def gossip(half):
        solve(half)

        def columns(tile, _):
            cols = pl.ds(pl.multiple_of(half * 512 + tile * 128, 128), 128)
            blocks = [RX[i, :, cols] for i in range(16)]
            first = mixed(0, half, blocks)
            second = mixed(1, half, [b + m for b, m in zip(blocks, first)])
            for i in range(16):
                NEW[i, :, cols] = first[i] + second[i]
            return 0

        lax.fori_loop(0, 4, columns, 0)
        cols = slice(half * 512, half * 512 + 512)
        for to in others:
            send(NEW.at[to, :, cols], o_move.at[here, cols], b_s.at[half], b_r.at[half], {"worker": to, "tok": flip})

    own(4)
    own(5)
    wait_rows(0)
    distances(0)
    pack(0)
    share_out(0, 0)
    finish(4)
    finish(5)
    finish_across(0)
    finish_across(1)
    put = pltpu.make_async_copy(GR, o_grad, g_s.at[0])
    put.start()
    add_up(0, 0)
    share_out(0, 1)
    wait_bytes(MR.at[0:15], m_r.at[0])
    wait_rows(1)
    distances(1)
    pack(1)
    share_out(1, 0)
    add_up(0, 1)
    gossip(0)
    add_up(1, 0)
    share_out(1, 1)
    add_up(1, 1)
    gossip(1)

    for cp in list(d.values()) + list(y1.values()) + list(y2.values()) + list(z.values()):
        cp.wait_send()
    for cp in list(zf.values()) + list(w1.values()) + list(w2.values()):
        cp.wait_send()
    wait_bytes(MR.at[0:15], m_s.at[0])
    for half in range(2):
        for stage, got in enumerate((R1, R2)):
            wait_bytes(got.at[half, :, 0:2], r_s.at[half, stage])
    for k in range(8):
        wait_bytes(CUR.at[:, k * 128 : k * 128 + 128], a_s.at[k])
    put.wait()
    for half in range(2):
        cols = slice(half * 512, half * 512 + 512)
        wait_bytes(NEW.at[:, :, cols], b_s.at[half])
        wait_bytes(o_move.at[:, cols], b_r.at[half])


def per_device(inputs, cotangent, weights, momentum, mix_weights, clip_radius):
    vmem = pl.BlockSpec(memory_space=pltpu.VMEM)
    hbm = pl.BlockSpec(memory_space=pl.ANY)
    dma = pltpu.SemaphoreType.DMA
    block = jax.ShapeDtypeStruct((128, 1024), F32)
    moved, gradient = pl.pallas_call(
        kernel,
        out_shape=(block, block),
        in_specs=[hbm, hbm, hbm, hbm, vmem, pl.BlockSpec(memory_space=pltpu.SMEM)],
        out_specs=(hbm, hbm),
        scratch_shapes=[
            pltpu.VMEM((8, 1536, 256), BF16),
            pltpu.VMEM((4, 1536, 256), BF16),
            pltpu.VMEM((2, 2, 4, 8, 128, 128), F32),
            pltpu.VMEM((2, 4, 8, 128, 128), F32),
            pltpu.VMEM((6, 2, 128, 128), F32),
            pltpu.VMEM((2, 6, 2, 128, 128), F32),
            pltpu.VMEM((6, 128, 128), F32),
            pltpu.VMEM((4, 2, 128, 128), F32),
            pltpu.VMEM((2, 128, 128), F32),
            pltpu.VMEM((2, 2, 128, 128), F32),
            pltpu.VMEM((128, 1024), F32),
            pltpu.VMEM((128, 1024), F32),
            pltpu.VMEM((128, 1024), F32),
            pltpu.VMEM((128, 1024), F32),
            pltpu.VMEM((16, 8, 1024), F32),
            pltpu.VMEM((16, 8, 1024), F32),
            pltpu.VMEM((512, 128), F32),
            pltpu.VMEM((2, 3, 8, 128), F32),
            pltpu.VMEM((2, 15, 8, 128), F32),
            pltpu.VMEM((2, 15, 8, 128), F32),
            pltpu.VMEM((8, 128), F32),
            pltpu.VMEM((16, 8, 128), F32),
            pltpu.VMEM((2, 4, 32, 128), F32),
            dma((14,)),
            dma((10,)), dma((10,)),
            dma((6,)), dma((6,)),
            dma((2, 6)), dma((2, 6)),
            dma((6,)), dma((6,)),
            dma((4,)), dma((4,)),
            dma((2,)), dma((2,)),
            dma((2, 2)), dma((2, 2)),
            dma((8,)), dma((8,)),
            dma((1,)), dma((1,)),
            dma((2, 2)), dma((2, 2)),
            dma((2,)), dma((2,)),
            dma((1,)),
            pltpu.SemaphoreType.REGULAR((4,)),
        ],
        compiler_params=pltpu.CompilerParams(
            collective_id=0, has_side_effects=True, vmem_limit_bytes=56 * 1024 * 1024
        ),
    )(inputs[0], cotangent[0], weights[0], momentum[0], mix_weights, clip_radius)
    velocity = 0.5 * momentum[0] + gradient
    new = (weights[0] - LEARNING_RATE * velocity) + moved
    return (new[None], velocity[None])


def solution(mesh):
    placed = (
        P("worker", "tok", None),
        P("worker", "tok", None),
        P("worker", "tok", None),
        P("worker", "tok", None),
        P("worker", None),
        P(),
    )
    return jax.shard_map(
        per_device,
        mesh=mesh,
        in_specs=placed,
        out_specs=(P("worker", "tok", None), P("worker", "tok", None)),
        check_vma=False,
    )
```

```python
import math

import jax
import jax.numpy as jnp
from jax import lax
from jax.experimental import pallas as pl
from jax.experimental.pallas import tpu as pltpu
from jax.sharding import PartitionSpec as P

D = 2048
KV_WIDTH = 512
ROUNDS = 2
LEARNING_RATE = 0.25

MESH = pl.DeviceIdType.MESH
F32 = jnp.float32
BF16 = jnp.bfloat16
HIGHEST = lax.Precision.HIGHEST

ORDER = ((1, 2), (0, 2), (1, 1), (0, 1), (1, 3), (0, 3), (1, 0), (0, 0))
PAIRS = 3


def kernel(
    feat, cot, wts, mom, mix, clip, o_move, o_grad,
    F, C, PA, PR, Y1, Y2, ZR, ZF, W1, W2, WT, MO, CUR, GR, RX, NEW, DP, PAY, R1, R2, MS, MR, SH, KC,
    ld, d_s, d_r, y1_s, y1_r, y2_s, y2_r, z_s, z_r, zf_s, zf_r, w1_s, w1_r, w2_s, w2_r,
    a_s, a_r, m_s, m_r, r_s, r_r, b_s, b_r, g_s, far,
):
    t = lax.axis_index("tok")
    w = lax.axis_index("worker")
    q, y, c = lax.div(t, 8), lax.rem(lax.div(t, 2), 4), lax.rem(t, 2)

    def load(src, dst, i):
        cp = pltpu.make_async_copy(src, dst, ld.at[i])
        cp.start()
        return cp

    def feat_block(j):
        dq, dy = ORDER[j]
        chip = (1 - q if dq else q) * 4 + lax.rem(y + dy, 4)
        return feat.at[:, pl.ds(pl.multiple_of(chip * 256, 256), 256)]

    def load_feat(j):
        f_loads[j] = load(feat_block(j), F.at[j], j)

    def load_cot(n):
        c_loads[n] = load(cot.at[:, n * 256 : (n + 1) * 256], C.at[n], 8 + n)

    f_loads, c_loads = {}, {}
    load_feat(0)
    load_cot(0)
    load_feat(1)

    def chip_at(z, y, c):
        return z * 8 + y * 2 + c

    h, x = lax.div(w, 4), lax.rem(w, 4)
    ys = [y] + [lax.rem(y + i, 4) for i in range(1, 4)]
    hs = [h] + [lax.rem(h + i, 4) for i in range(1, 4)]
    xs = [x] + [lax.rem(x + i, 4) for i in range(1, 4)]
    flip = chip_at(1 - q, y, c)
    sibling = {"worker": w, "tok": chip_at(q, y, 1 - c)}
    up = {"worker": w, "tok": chip_at(q, ys[1], c)}
    down = {"worker": w, "tok": chip_at(q, ys[3], c)}
    across = {"worker": w, "tok": flip}
    beyond = lax.rem(h + 2 * q + 3, 4)
    next_to = [sibling, up, down, across] + [
        {"worker": h * 4 + xs[1], "tok": t},
        {"worker": h * 4 + xs[3], "tok": t},
        {"worker": beyond * 4 + x, "tok": flip},
    ]
    barrier = pltpu.get_barrier_semaphore()
    for peer in next_to:
        pl.semaphore_signal(barrier, inc=1, device_id=peer, device_id_type=MESH)

    def tell(n):
        for peer in next_to:
            pl.semaphore_signal(far.at[n], inc=1, device_id=peer, device_id_type=MESH)

    def heard(n):
        pl.semaphore_wait(far.at[n], 7)

    def send(src, dst, ss, rs, peer):
        cp = pltpu.make_async_remote_copy(
            src_ref=src, dst_ref=dst, send_sem=ss, recv_sem=rs, device_id=peer, device_id_type=MESH
        )
        cp.start()
        return cp

    def wait_bytes(ref, sem):
        pltpu.make_async_copy(ref, ref, sem).wait()

    mine = PA.at[c]

    def product(j, n):
        dq, dy = ORDER[j]
        r = lax.dot_general(F[j], C[n], (((0,), (0,)), ((), ())), preferred_element_type=F32)
        for core in range(2):
            for k in range(2):
                PA[core, dq, dy, 2 * n + k] = r[core * 128 : core * 128 + 128, k * 128 : k * 128 + 128]

    d, zf, y1 = {}, {}, {}

    def first_across(dy):
        zf[dy] = send(mine.at[1, dy, 6:8], ZF.at[dy], zf_s.at[dy], zf_r.at[dy], across)

    def opposite(n):
        d[n].wait_recv()
        for dq in range(2):
            for k in (2 * n, 2 * n + 1):
                mine[dq, 2, k] = mine[dq, 2, k] + PR[dq, 2, k]
        if n < PAIRS:
            for k in (2 * n, 2 * n + 1):
                y1[k] = send(mine.at[:, 2, k], Y1.at[k], y1_s.at[k], y1_r.at[k], (up, down)[k % 2])
        else:
            first_across(2)

    for n in range(4):
        for j in range(2):
            if n == 0 and j == 0:
                load_cot(1)
            if n == 0:
                f_loads[j].wait()
            if j == 0:
                c_loads[n].wait()
            if n == 0 and j == 0:
                load_cot(2)
            product(j, n)
        if n == 0:
            load_cot(3)
            load_feat(2)
            pl.semaphore_wait(barrier, 7)
        else:
            load_feat(2 * n + 1)
            if n < 3:
                load_feat(2 * n + 2)
        d[n] = send(PA.at[1 - c, :, 2, 2 * n : 2 * n + 2], PR.at[:, 2, 2 * n : 2 * n + 2], d_s.at[n], d_r.at[n], sibling)
        if n >= 1:
            opposite(n - 1)
    w_load, m_load = load(wts, WT, 12), load(mom, MO, 13)
    tell(0)
    tok_peers = [
        {"worker": w, "tok": chip_at(z_at, ys[dy], core)}
        for dy in (2, 1, 3, 0) for z_at in (1 - q, q) for core in (1 - c, c)
    ][:-1]
    others = [hs[dh] * 4 + xs[dx] for dx in (2, 1, 3, 0) for dh in (2, 1, 3, 0)]
    work_peers = [{"worker": other, "tok": flip} for other in others[:-1]]

    def add_sibling(j):
        dq, dy = ORDER[j]
        d[j + 2].wait_recv()
        mine[dq, dy] = mine[dq, dy] + PR[dq, dy]
        if dq == 1:
            first_across(dy)

    y2 = {}

    def along(side, k):
        to, dy = ((up, 1), (down, 3))[side]
        y2[side, k] = send(mine.at[:, dy, k], Y2.at[side, k], y2_s.at[side, k], y2_r.at[side, k], to)

    def plain(k):
        along(1 - k % 2, k)

    def joined(k):
        side, dy = k % 2, (1, 3)[k % 2]
        y1[k].wait_recv()
        mine[:, dy, k] = mine[:, dy, k] + Y1[k]
        along(side, k)

    for j in range(2, 8):
        dq, dy = ORDER[j]
        f_loads[j].wait()
        for n in range(4):
            product(j, n)
        d[j + 2] = send(PA.at[1 - c, dq, dy], PR.at[dq, dy], d_s.at[j + 2], d_r.at[j + 2], sibling)
        if j == 2:
            opposite(3)
        else:
            add_sibling(j - 1)
        if j == 4:
            plain(1)
            heard(0)
            tell(1)
        if j == 6:
            plain(0)
            heard(1)
            tell(2)

    z = {}

    def own(k):
        y2[0, k].wait_recv()
        y2[1, k].wait_recv()
        mine[:, 0, k] = mine[:, 0, k] + Y2[0, k] + Y2[1, k]
        z[k] = send(mine.at[1, 0, k], ZR.at[k], z_s.at[k], z_r.at[k], across)

    def step(k, gradient):
        cols = slice(k * 128, k * 128 + 128)
        velocity = 0.5 * MO[:, cols] + gradient
        GR[:, cols] = gradient
        CUR[:, cols] = WT[:, cols] - LEARNING_RATE * velocity

    groups = ((0,), (1,), (2,), (3,), (4,), (5,), (6, 7))

    def columns_of(group):
        return slice(group[0] * 128, group[-1] * 128 + 128)

    def transpose_out(group):
        k, cols = group[0], columns_of(group)
        for to in others:
            rows = pl.ds(pl.multiple_of(to * 8, 8), 8)
            send(CUR.at[rows, cols], RX.at[w, :, cols], a_s.at[k], a_r.at[k], {"worker": to, "tok": flip})

    def leave(k):
        for group in groups:
            if group[-1] == k:
                transpose_out(group)

    def finish(k):
        z[k].wait_recv()
        step(k, mine[0, 0, k] + ZR[k])
        leave(k)

    w1, w2 = {}, {}

    def across_one():
        for dy in (2, 1, 3, 0):
            zf[dy].wait_recv()
            mine[0, dy, 6:8] = mine[0, dy, 6:8] + ZF[dy]
        for k in range(2):
            w1[k] = send(mine.at[0, 2, 6 + k], W1.at[k], w1_s.at[k], w1_r.at[k], (up, down)[k])

    def across_two(k):
        dy = (1, 3)[k]
        w1[k].wait_recv()
        mine[0, dy, 6 + k] = mine[0, dy, 6 + k] + W1[k]
        for side in range(2):
            w2[side, k] = send(
                mine.at[0, (1, 3)[side], 6 + k], W2.at[side, k], w2_s.at[side, k], w2_r.at[side, k], (up, down)[side]
            )

    def finish_across(k):
        for side in range(2):
            w2[side, k].wait_recv()
        step(6 + k, mine[0, 0, 6 + k] + W2[0, k] + W2[1, k])
        leave(6 + k)

    joined(0)
    joined(1)
    add_sibling(7)
    heard(2)
    tell(3)
    joined(2)
    plain(2)
    plain(3)
    joined(3)
    w_load.wait()
    m_load.wait()
    MS[...] = jnp.zeros_like(MS)
    MS[0:1, 0:5] = mix[...].astype(F32)
    MR[w] = MS[...]
    for half in range(2):
        for i in range(16):
            DP[half * 256 + i * 17 : half * 256 + i * 17 + 1, :] = jnp.zeros((1, 128), F32)
    heard(3)
    for peer in work_peers:
        send(MS, MR.at[w], m_s.at[0], m_r.at[0], peer)
    across_one()
    own(0)
    own(1)
    joined(4)
    plain(4)
    plain(5)
    joined(5)
    finish(0)
    finish(1)
    own(2)
    own(3)
    across_two(0)
    across_two(1)
    finish(2)
    finish(3)

    def distances(half):
        for bi in range(4):
            for bj in range(bi, 4):
                which = [(i, j) for i in range(4) for j in range(i + 1 if bi == bj else 0, 4)]

                def tiles(tile, acc, bi=bi, bj=bj, which=which):
                    cols = pl.ds(pl.multiple_of(half * 512 + tile * 128, 128), 128)
                    left = [RX[4 * bi + i, :, cols] for i in range(4)]
                    right = left if bi == bj else [RX[4 * bj + i, :, cols] for i in range(4)]
                    diffs = [left[i] - right[j] for i, j in which]
                    return tuple(a + e * e for a, e in zip(acc, diffs))

                acc = lax.fori_loop(0, 4, tiles, tuple(jnp.zeros((8, 128), F32) for _ in which))
                for (i, j), total in zip(which, acc):
                    row = jnp.sum(total, axis=0, keepdims=True)
                    for a, b in ((4 * bi + i, 4 * bj + j), (4 * bj + j, 4 * bi + i)):
                        at = half * 256 + a * 16 + b
                        DP[at : at + 1, :] = row

    def wait_rows(half):
        for group in groups:
            if group[0] // 4 == half:
                wait_bytes(RX.at[:, :, columns_of(group)], a_r.at[group[0]])

    def pack(half):
        packed = lax.dot_general(
            jnp.ones((8, 128), F32), DP[half * 256 : half * 256 + 256, :], (((1,), (1,)), ((), ())),
            precision=HIGHEST, preferred_element_type=F32,
        )
        for r in range(2):
            PAY[half, 0, r : r + 1, :] = packed[0:1, r * 128 : r * 128 + 128]

    stages = ((tok_peers, R1), (work_peers, R2))

    def share_out(half, stage):
        peers, got = stages[stage]
        for i, peer in enumerate(peers):
            send(PAY.at[half, stage, 0:2], got.at[half, i, 0:2], r_s.at[half, stage], r_r.at[half, stage], peer)

    def add_up(half, stage):
        got = stages[stage][1]
        wait_bytes(got.at[half, :, 0:2], r_r.at[half, stage])
        parts = [PAY[half, stage, 0:2]] + [got[half, i, 0:2] for i in range(15)]
        while len(parts) > 1:
            parts = [a + b for a, b in zip(parts[::2], parts[1::2])]
        PAY[half, stage + 1, 0:2] = parts[0]

    def constants():
        row = lax.broadcasted_iota(jnp.int32, (16, 128), 0)
        lane = lax.broadcasted_iota(jnp.int32, (16, 128), 1)
        masks = [(lane == other).astype(F32) for other in (row ^ 1, row ^ 2, (row + 12) & 15, (row + 4) & 15)]
        from_lane = lax.broadcasted_iota(jnp.int32, (128, 128), 0)
        to_lane = lax.broadcasted_iota(jnp.int32, (128, 128), 1)
        pick = ((from_lane & 15) == to_lane).astype(F32)
        return (lane >> 4) == (row & 7), masks, (lane == row).astype(F32), pick

    def take_shares():
        lane = lax.broadcasted_iota(jnp.int32, (16, 128), 1)
        mixing = MR[:, 0, :]
        shares = mixing / jnp.sum(mixing, axis=1, keepdims=True)
        for k in range(4):
            share = jnp.sum(jnp.where(lane == k + 1, shares, 0.0), axis=1, keepdims=True)
            SH[k] = jnp.broadcast_to(share, (16, 128))

    def solve(half):
        place, masks, eye, pick = constants()
        spread = jnp.concatenate([jnp.broadcast_to(PAY[half, 2, r : r + 1, :], (8, 128)) for r in range(2)], axis=0)
        dist2 = jnp.dot(jnp.where(place, spread, 0.0), pick, precision=HIGHEST, preferred_element_type=F32)
        pad = jnp.zeros((112, 128), F32)
        for round_index in range(ROUNDS):
            radius = clip[round_index].astype(F32) * (math.sqrt(D * KV_WIDTH) / 1000.0)
            moves = []
            for k in range(4):
                squares = jnp.sum(dist2 * masks[k], axis=1, keepdims=True)
                factor = radius / jnp.maximum(jnp.sqrt(jnp.maximum(squares, 0.0)), radius)
                moves.append(SH[k] * factor)
                KC[round_index, k, half * 16 : half * 16 + 16, :] = moves[k]
            if round_index == 0:
                mixer = eye * (1.0 - (moves[0] + moves[1] + moves[2] + moves[3]))
                for k in range(4):
                    mixer = mixer + masks[k] * moves[k]
                left = jnp.dot(
                    mixer, jnp.concatenate([dist2, pad], axis=0), precision=HIGHEST, preferred_element_type=F32
                )
                both = lax.dot_general(
                    left, jnp.concatenate([mixer, pad], axis=0), (((1,), (1,)), ((), ())),
                    precision=HIGHEST, preferred_element_type=F32,
                )
                diagonal = both * eye
                by_row = jnp.sum(diagonal, axis=1, keepdims=True)
                by_lane = jnp.sum(diagonal, axis=0, keepdims=True)
                dist2 = both - 0.5 * (by_row + by_lane)

    neighbours = [(i ^ 1, i ^ 2, (i - 4) % 16, (i + 4) % 16) for i in range(16)]

    def mixed(round_index, half, blocks):
        out = []
        for i in range(16):
            moved = None
            for k, j in enumerate(neighbours[i]):
                by = jnp.broadcast_to(KC[round_index, k, half * 16 + i : half * 16 + i + 1, :], (8, 128))
                term = by * (blocks[j] - blocks[i])
                moved = term if moved is None else moved + term
            out.append(moved)
        return out

    here = pl.ds(pl.multiple_of(w * 8, 8), 8)

    def mix_rows(half):

        def columns(tile, _):
            cols = pl.ds(pl.multiple_of(half * 512 + tile * 128, 128), 128)
            blocks = [RX[i, :, cols] for i in range(16)]
            first = mixed(0, half, blocks)
            second = mixed(1, half, [b + m for b, m in zip(blocks, first)])
            for i in range(16):
                NEW[i, :, cols] = first[i] + second[i]
            return 0

        lax.fori_loop(0, 4, columns, 0)
        cols = slice(half * 512, half * 512 + 512)
        for to in others:
            send(NEW.at[to, :, cols], o_move.at[here, cols], b_s.at[half], b_r.at[half], {"worker": to, "tok": flip})

    own(4)
    own(5)
    wait_rows(0)
    distances(0)
    pack(0)
    share_out(0, 0)
    finish(4)
    finish_across(0)
    finish(5)
    finish_across(1)
    put = pltpu.make_async_copy(GR, o_grad, g_s.at[0])
    put.start()
    add_up(0, 0)
    share_out(0, 1)
    wait_bytes(MR.at[0:15], m_r.at[0])
    take_shares()
    wait_rows(1)
    distances(1)
    pack(1)
    share_out(1, 0)
    add_up(0, 1)
    solve(0)
    mix_rows(0)
    add_up(1, 0)
    share_out(1, 1)
    add_up(1, 1)
    solve(1)
    mix_rows(1)

    for cp in list(d.values()) + list(y1.values()) + list(y2.values()) + list(z.values()):
        cp.wait_send()
    for cp in list(zf.values()) + list(w1.values()) + list(w2.values()):
        cp.wait_send()
    wait_bytes(MR.at[0:15], m_s.at[0])
    for half in range(2):
        for stage, got in enumerate((R1, R2)):
            wait_bytes(got.at[half, :, 0:2], r_s.at[half, stage])
    for group in groups:
        wait_bytes(CUR.at[:, columns_of(group)], a_s.at[group[0]])
    put.wait()
    for half in range(2):
        cols = slice(half * 512, half * 512 + 512)
        wait_bytes(NEW.at[:, :, cols], b_s.at[half])
        wait_bytes(o_move.at[:, cols], b_r.at[half])


def per_device(inputs, cotangent, weights, momentum, mix_weights, clip_radius):
    vmem = pl.BlockSpec(memory_space=pltpu.VMEM)
    hbm = pl.BlockSpec(memory_space=pl.ANY)
    dma = pltpu.SemaphoreType.DMA
    block = jax.ShapeDtypeStruct((128, 1024), F32)
    moved, gradient = pl.pallas_call(
        kernel,
        out_shape=(block, block),
        in_specs=[hbm, hbm, hbm, hbm, vmem, pl.BlockSpec(memory_space=pltpu.SMEM)],
        out_specs=(hbm, hbm),
        scratch_shapes=[
            pltpu.VMEM((8, 1536, 256), BF16),
            pltpu.VMEM((4, 1536, 256), BF16),
            pltpu.VMEM((2, 2, 4, 8, 128, 128), F32),
            pltpu.VMEM((2, 4, 8, 128, 128), F32),
            pltpu.VMEM((6, 2, 128, 128), F32),
            pltpu.VMEM((2, 6, 2, 128, 128), F32),
            pltpu.VMEM((6, 128, 128), F32),
            pltpu.VMEM((4, 2, 128, 128), F32),
            pltpu.VMEM((2, 128, 128), F32),
            pltpu.VMEM((2, 2, 128, 128), F32),
            pltpu.VMEM((128, 1024), F32),
            pltpu.VMEM((128, 1024), F32),
            pltpu.VMEM((128, 1024), F32),
            pltpu.VMEM((128, 1024), F32),
            pltpu.VMEM((16, 8, 1024), F32),
            pltpu.VMEM((16, 8, 1024), F32),
            pltpu.VMEM((512, 128), F32),
            pltpu.VMEM((2, 3, 8, 128), F32),
            pltpu.VMEM((2, 15, 8, 128), F32),
            pltpu.VMEM((2, 15, 8, 128), F32),
            pltpu.VMEM((8, 128), F32),
            pltpu.VMEM((16, 8, 128), F32),
            pltpu.VMEM((4, 16, 128), F32),
            pltpu.VMEM((2, 4, 32, 128), F32),
            dma((14,)),
            dma((10,)), dma((10,)),
            dma((6,)), dma((6,)),
            dma((2, 6)), dma((2, 6)),
            dma((6,)), dma((6,)),
            dma((4,)), dma((4,)),
            dma((2,)), dma((2,)),
            dma((2, 2)), dma((2, 2)),
            dma((8,)), dma((8,)),
            dma((1,)), dma((1,)),
            dma((2, 2)), dma((2, 2)),
            dma((2,)), dma((2,)),
            dma((1,)),
            pltpu.SemaphoreType.REGULAR((4,)),
        ],
        compiler_params=pltpu.CompilerParams(
            collective_id=0, has_side_effects=True, vmem_limit_bytes=56 * 1024 * 1024
        ),
    )(inputs[0], cotangent[0], weights[0], momentum[0], mix_weights, clip_radius)
    velocity = 0.5 * momentum[0] + gradient
    new = (weights[0] - LEARNING_RATE * velocity) + moved
    return (new[None], velocity[None])


def solution(mesh):
    placed = (
        P("worker", "tok", None),
        P("worker", "tok", None),
        P("worker", "tok", None),
        P("worker", "tok", None),
        P("worker", None),
        P(),
    )
    return jax.shard_map(
        per_device,
        mesh=mesh,
        in_specs=placed,
        out_specs=(P("worker", "tok", None), P("worker", "tok", None)),
        check_vma=False,
    )
```

```python
import math

import jax
import jax.numpy as jnp
from jax import lax
from jax.experimental import pallas as pl
from jax.experimental.pallas import tpu as pltpu
from jax.sharding import PartitionSpec as P

D = 2048
KV_WIDTH = 512
ROUNDS = 2
LEARNING_RATE = 0.25

MESH = pl.DeviceIdType.MESH
F32 = jnp.float32
BF16 = jnp.bfloat16
HIGHEST = lax.Precision.HIGHEST

ORDER = ((1, 2), (0, 2), (1, 1), (0, 1), (1, 3), (0, 3), (1, 0), (0, 0))
PAIRS = 3


def kernel(
    feat, cot, wts, mom, mix, clip, o_move, o_grad,
    F, C, PA, PR, Y1, Y2, ZR, ZF, W1, W2, WT, MO, CUR, GR, RX, NEW, DP, PAY, R1, R2, MS, MR, SH, KC,
    ld, d_s, d_r, y1_s, y1_r, y2_s, y2_r, z_s, z_r, zf_s, zf_r, w1_s, w1_r, w2_s, w2_r,
    a_s, a_r, m_s, m_r, r_s, r_r, b_s, b_r, g_s, far,
):
    t = lax.axis_index("tok")
    w = lax.axis_index("worker")
    q, y, c = lax.div(t, 8), lax.rem(lax.div(t, 2), 4), lax.rem(t, 2)

    def load(src, dst, i):
        cp = pltpu.make_async_copy(src, dst, ld.at[i])
        cp.start()
        return cp

    def feat_block(j):
        dq, dy = ORDER[j]
        chip = (1 - q if dq else q) * 4 + lax.rem(y + dy, 4)
        return feat.at[:, pl.ds(pl.multiple_of(chip * 256, 256), 256)]

    def load_feat(j):
        f_loads[j] = load(feat_block(j), F.at[j], j)

    def load_cot(n):
        c_loads[n] = load(cot.at[:, n * 256 : (n + 1) * 256], C.at[n], 8 + n)

    f_loads, c_loads = {}, {}
    load_feat(0)
    load_cot(0)
    load_feat(1)

    def chip_at(z, y, c):
        return z * 8 + y * 2 + c

    h, x = lax.div(w, 4), lax.rem(w, 4)
    ys = [y] + [lax.rem(y + i, 4) for i in range(1, 4)]
    hs = [h] + [lax.rem(h + i, 4) for i in range(1, 4)]
    xs = [x] + [lax.rem(x + i, 4) for i in range(1, 4)]
    flip = chip_at(1 - q, y, c)
    sibling = {"worker": w, "tok": chip_at(q, y, 1 - c)}
    up = {"worker": w, "tok": chip_at(q, ys[1], c)}
    down = {"worker": w, "tok": chip_at(q, ys[3], c)}
    across = {"worker": w, "tok": flip}
    beyond = lax.rem(h + 2 * q + 3, 4)
    next_to = [sibling, up, down, across] + [
        {"worker": h * 4 + xs[1], "tok": t},
        {"worker": h * 4 + xs[3], "tok": t},
        {"worker": beyond * 4 + x, "tok": flip},
    ]
    barrier = pltpu.get_barrier_semaphore()
    for peer in next_to:
        pl.semaphore_signal(barrier, inc=1, device_id=peer, device_id_type=MESH)

    def tell(n):
        for peer in next_to:
            pl.semaphore_signal(far.at[n], inc=1, device_id=peer, device_id_type=MESH)

    def heard(n):
        pl.semaphore_wait(far.at[n], 7)

    def send(src, dst, ss, rs, peer):
        cp = pltpu.make_async_remote_copy(
            src_ref=src, dst_ref=dst, send_sem=ss, recv_sem=rs, device_id=peer, device_id_type=MESH
        )
        cp.start()
        return cp

    def wait_bytes(ref, sem):
        pltpu.make_async_copy(ref, ref, sem).wait()

    mine = PA.at[c]

    def product(j, n):
        dq, dy = ORDER[j]
        r = lax.dot_general(F[j], C[n], (((0,), (0,)), ((), ())), preferred_element_type=F32)
        for core in range(2):
            for k in range(2):
                PA[core, dq, dy, 2 * n + k] = r[core * 128 : core * 128 + 128, k * 128 : k * 128 + 128]

    d, zf, y1 = {}, {}, {}

    def first_across(dy):
        zf[dy] = send(mine.at[1, dy, 6:8], ZF.at[dy], zf_s.at[dy], zf_r.at[dy], across)

    def opposite(n):
        d[n].wait_recv()
        for dq in range(2):
            for k in (2 * n, 2 * n + 1):
                mine[dq, 2, k] = mine[dq, 2, k] + PR[dq, 2, k]
        if n < PAIRS:
            for k in (2 * n, 2 * n + 1):
                y1[k] = send(mine.at[:, 2, k], Y1.at[k], y1_s.at[k], y1_r.at[k], (up, down)[k % 2])
        else:
            first_across(2)

    for n in range(4):
        for j in range(2):
            if n == 0 and j == 0:
                load_cot(1)
            if n == 0:
                f_loads[j].wait()
            if j == 0:
                c_loads[n].wait()
            if n == 0 and j == 0:
                load_cot(2)
                load_cot(3)
                load_feat(2)
            product(j, n)
        if n == 0:
            load_feat(3)
            load_feat(4)
            load_feat(5)
            pl.semaphore_wait(barrier, 7)
        elif n == 1:
            load_feat(6)
            load_feat(7)
        d[n] = send(PA.at[1 - c, :, 2, 2 * n : 2 * n + 2], PR.at[:, 2, 2 * n : 2 * n + 2], d_s.at[n], d_r.at[n], sibling)
        if n >= 1:
            opposite(n - 1)
    w_load, m_load = load(wts, WT, 12), load(mom, MO, 13)
    tell(0)
    tok_peers = [
        {"worker": w, "tok": chip_at(z_at, ys[dy], core)}
        for dy in (2, 1, 3, 0) for z_at in (1 - q, q) for core in (1 - c, c)
    ][:-1]
    others = [hs[dh] * 4 + xs[dx] for dx in (2, 1, 3, 0) for dh in (2, 1, 3, 0)]
    work_peers = [{"worker": other, "tok": flip} for other in others[:-1]]

    def add_sibling(j):
        dq, dy = ORDER[j]
        d[j + 2].wait_recv()
        mine[dq, dy] = mine[dq, dy] + PR[dq, dy]
        if dq == 1:
            first_across(dy)

    y2 = {}

    def along(side, k):
        to, dy = ((up, 1), (down, 3))[side]
        y2[side, k] = send(mine.at[:, dy, k], Y2.at[side, k], y2_s.at[side, k], y2_r.at[side, k], to)

    def plain(k):
        along(1 - k % 2, k)

    def joined(k):
        side, dy = k % 2, (1, 3)[k % 2]
        y1[k].wait_recv()
        mine[:, dy, k] = mine[:, dy, k] + Y1[k]
        along(side, k)

    for j in range(2, 8):
        dq, dy = ORDER[j]
        f_loads[j].wait()
        for n in range(4):
            product(j, n)
        d[j + 2] = send(PA.at[1 - c, dq, dy], PR.at[dq, dy], d_s.at[j + 2], d_r.at[j + 2], sibling)
        if j == 2:
            opposite(3)
        else:
            add_sibling(j - 1)
        if j == 4:
            plain(1)
            heard(0)
            tell(1)
        if j == 6:
            plain(0)
            heard(1)
            tell(2)

    z = {}

    def own(k):
        y2[0, k].wait_recv()
        y2[1, k].wait_recv()
        mine[:, 0, k] = mine[:, 0, k] + Y2[0, k] + Y2[1, k]
        z[k] = send(mine.at[1, 0, k], ZR.at[k], z_s.at[k], z_r.at[k], across)

    def step(k, gradient):
        cols = slice(k * 128, k * 128 + 128)
        velocity = 0.5 * MO[:, cols] + gradient
        GR[:, cols] = gradient
        CUR[:, cols] = WT[:, cols] - LEARNING_RATE * velocity

    groups = ((0,), (1,), (2,), (3,), (4,), (5,), (6, 7))

    def columns_of(group):
        return slice(group[0] * 128, group[-1] * 128 + 128)

    def transpose_out(group):
        k, cols = group[0], columns_of(group)
        for to in others:
            rows = pl.ds(pl.multiple_of(to * 8, 8), 8)
            send(CUR.at[rows, cols], RX.at[w, :, cols], a_s.at[k], a_r.at[k], {"worker": to, "tok": flip})

    def leave(k):
        for group in groups:
            if group[-1] == k:
                transpose_out(group)

    def finish(k):
        z[k].wait_recv()
        step(k, mine[0, 0, k] + ZR[k])
        leave(k)

    w1, w2 = {}, {}

    def across_one():
        for dy in (2, 1, 3, 0):
            zf[dy].wait_recv()
            mine[0, dy, 6:8] = mine[0, dy, 6:8] + ZF[dy]
        for k in range(2):
            w1[k] = send(mine.at[0, 2, 6 + k], W1.at[k], w1_s.at[k], w1_r.at[k], (up, down)[k])

    def across_two(k):
        dy = (1, 3)[k]
        w1[k].wait_recv()
        mine[0, dy, 6 + k] = mine[0, dy, 6 + k] + W1[k]
        for side in range(2):
            w2[side, k] = send(
                mine.at[0, (1, 3)[side], 6 + k], W2.at[side, k], w2_s.at[side, k], w2_r.at[side, k], (up, down)[side]
            )

    def finish_across(k):
        for side in range(2):
            w2[side, k].wait_recv()
        step(6 + k, mine[0, 0, 6 + k] + W2[0, k] + W2[1, k])
        leave(6 + k)

    joined(0)
    joined(1)
    add_sibling(7)
    heard(2)
    tell(3)
    joined(2)
    plain(2)
    plain(3)
    joined(3)
    w_load.wait()
    m_load.wait()
    MS[...] = jnp.zeros_like(MS)
    MS[0:1, 0:5] = mix[...].astype(F32)
    MR[w] = MS[...]
    for half in range(2):
        for i in range(16):
            DP[half * 256 + i * 17 : half * 256 + i * 17 + 1, :] = jnp.zeros((1, 128), F32)
    heard(3)
    for peer in work_peers:
        send(MS, MR.at[w], m_s.at[0], m_r.at[0], peer)
    across_one()
    own(0)
    own(1)
    joined(4)
    plain(4)
    plain(5)
    joined(5)
    finish(0)
    finish(1)
    own(2)
    own(3)
    across_two(0)
    across_two(1)
    finish(2)
    finish(3)

    def distances(half):
        for bi in range(4):
            for bj in range(bi, 4):
                which = [(i, j) for i in range(4) for j in range(i + 1 if bi == bj else 0, 4)]

                def tiles(tile, acc, bi=bi, bj=bj, which=which):
                    cols = pl.ds(pl.multiple_of(half * 512 + tile * 128, 128), 128)
                    left = [RX[4 * bi + i, :, cols] for i in range(4)]
                    right = left if bi == bj else [RX[4 * bj + i, :, cols] for i in range(4)]
                    diffs = [left[i] - right[j] for i, j in which]
                    return tuple(a + e * e for a, e in zip(acc, diffs))

                acc = lax.fori_loop(0, 4, tiles, tuple(jnp.zeros((8, 128), F32) for _ in which))
                for (i, j), total in zip(which, acc):
                    row = jnp.sum(total, axis=0, keepdims=True)
                    for a, b in ((4 * bi + i, 4 * bj + j), (4 * bj + j, 4 * bi + i)):
                        at = half * 256 + a * 16 + b
                        DP[at : at + 1, :] = row

    def wait_rows(half):
        for group in groups:
            if group[0] // 4 == half:
                wait_bytes(RX.at[:, :, columns_of(group)], a_r.at[group[0]])

    def pack(half):
        packed = lax.dot_general(
            jnp.ones((8, 128), F32), DP[half * 256 : half * 256 + 256, :], (((1,), (1,)), ((), ())),
            precision=HIGHEST, preferred_element_type=F32,
        )
        for r in range(2):
            PAY[half, 0, r : r + 1, :] = packed[0:1, r * 128 : r * 128 + 128]

    stages = ((tok_peers, R1), (work_peers, R2))

    def share_out(half, stage):
        peers, got = stages[stage]
        for i, peer in enumerate(peers):
            send(PAY.at[half, stage, 0:2], got.at[half, i, 0:2], r_s.at[half, stage], r_r.at[half, stage], peer)

    def add_up(half, stage):
        got = stages[stage][1]
        wait_bytes(got.at[half, :, 0:2], r_r.at[half, stage])
        parts = [PAY[half, stage, 0:2]] + [got[half, i, 0:2] for i in range(15)]
        while len(parts) > 1:
            parts = [a + b for a, b in zip(parts[::2], parts[1::2])]
        PAY[half, stage + 1, 0:2] = parts[0]

    def constants():
        row = lax.broadcasted_iota(jnp.int32, (16, 128), 0)
        lane = lax.broadcasted_iota(jnp.int32, (16, 128), 1)
        masks = [(lane == other).astype(F32) for other in (row ^ 1, row ^ 2, (row + 12) & 15, (row + 4) & 15)]
        from_lane = lax.broadcasted_iota(jnp.int32, (128, 128), 0)
        to_lane = lax.broadcasted_iota(jnp.int32, (128, 128), 1)
        pick = ((from_lane & 15) == to_lane).astype(F32)
        return (lane >> 4) == (row & 7), masks, (lane == row).astype(F32), pick

    def take_shares():
        lane = lax.broadcasted_iota(jnp.int32, (16, 128), 1)
        mixing = MR[:, 0, :]
        shares = mixing / jnp.sum(mixing, axis=1, keepdims=True)
        for k in range(4):
            share = jnp.sum(jnp.where(lane == k + 1, shares, 0.0), axis=1, keepdims=True)
            SH[k] = jnp.broadcast_to(share, (16, 128))

    def solve(half):
        place, masks, eye, pick = constants()
        spread = jnp.concatenate([jnp.broadcast_to(PAY[half, 2, r : r + 1, :], (8, 128)) for r in range(2)], axis=0)
        dist2 = jnp.dot(jnp.where(place, spread, 0.0), pick, precision=HIGHEST, preferred_element_type=F32)
        pad = jnp.zeros((112, 128), F32)
        for round_index in range(ROUNDS):
            radius = clip[round_index].astype(F32) * (math.sqrt(D * KV_WIDTH) / 1000.0)
            moves = []
            for k in range(4):
                squares = jnp.sum(dist2 * masks[k], axis=1, keepdims=True)
                factor = radius / jnp.maximum(jnp.sqrt(jnp.maximum(squares, 0.0)), radius)
                moves.append(SH[k] * factor)
                KC[round_index, k, half * 16 : half * 16 + 16, :] = moves[k]
            if round_index == 0:
                mixer = eye * (1.0 - (moves[0] + moves[1] + moves[2] + moves[3]))
                for k in range(4):
                    mixer = mixer + masks[k] * moves[k]
                left = jnp.dot(
                    mixer, jnp.concatenate([dist2, pad], axis=0), precision=HIGHEST, preferred_element_type=F32
                )
                both = lax.dot_general(
                    left, jnp.concatenate([mixer, pad], axis=0), (((1,), (1,)), ((), ())),
                    precision=HIGHEST, preferred_element_type=F32,
                )
                diagonal = both * eye
                by_row = jnp.sum(diagonal, axis=1, keepdims=True)
                by_lane = jnp.sum(diagonal, axis=0, keepdims=True)
                dist2 = both - 0.5 * (by_row + by_lane)

    neighbours = [(i ^ 1, i ^ 2, (i - 4) % 16, (i + 4) % 16) for i in range(16)]

    def mixed(round_index, half, blocks):
        out = []
        for i in range(16):
            moved = None
            for k, j in enumerate(neighbours[i]):
                by = jnp.broadcast_to(KC[round_index, k, half * 16 + i : half * 16 + i + 1, :], (8, 128))
                term = by * (blocks[j] - blocks[i])
                moved = term if moved is None else moved + term
            out.append(moved)
        return out

    here = pl.ds(pl.multiple_of(w * 8, 8), 8)

    def mix_rows(half):

        def columns(tile, _):
            cols = pl.ds(pl.multiple_of(half * 512 + tile * 128, 128), 128)
            blocks = [RX[i, :, cols] for i in range(16)]
            first = mixed(0, half, blocks)
            second = mixed(1, half, [b + m for b, m in zip(blocks, first)])
            for i in range(16):
                NEW[i, :, cols] = first[i] + second[i]
            return 0

        lax.fori_loop(0, 4, columns, 0)
        cols = slice(half * 512, half * 512 + 512)
        for to in others:
            send(NEW.at[to, :, cols], o_move.at[here, cols], b_s.at[half], b_r.at[half], {"worker": to, "tok": flip})

    own(4)
    own(5)
    wait_rows(0)
    distances(0)
    pack(0)
    share_out(0, 0)
    finish(4)
    finish_across(0)
    finish(5)
    finish_across(1)
    put = pltpu.make_async_copy(GR, o_grad, g_s.at[0])
    put.start()
    add_up(0, 0)
    share_out(0, 1)
    wait_bytes(MR.at[0:15], m_r.at[0])
    take_shares()
    wait_rows(1)
    distances(1)
    pack(1)
    share_out(1, 0)
    add_up(0, 1)
    solve(0)
    mix_rows(0)
    add_up(1, 0)
    share_out(1, 1)
    add_up(1, 1)
    solve(1)
    mix_rows(1)

    for cp in list(d.values()) + list(y1.values()) + list(y2.values()) + list(z.values()):
        cp.wait_send()
    for cp in list(zf.values()) + list(w1.values()) + list(w2.values()):
        cp.wait_send()
    wait_bytes(MR.at[0:15], m_s.at[0])
    for half in range(2):
        for stage, got in enumerate((R1, R2)):
            wait_bytes(got.at[half, :, 0:2], r_s.at[half, stage])
    for group in groups:
        wait_bytes(CUR.at[:, columns_of(group)], a_s.at[group[0]])
    put.wait()
    for half in range(2):
        cols = slice(half * 512, half * 512 + 512)
        wait_bytes(NEW.at[:, :, cols], b_s.at[half])
        wait_bytes(o_move.at[:, cols], b_r.at[half])


def per_device(inputs, cotangent, weights, momentum, mix_weights, clip_radius):
    vmem = pl.BlockSpec(memory_space=pltpu.VMEM)
    hbm = pl.BlockSpec(memory_space=pl.ANY)
    dma = pltpu.SemaphoreType.DMA
    block = jax.ShapeDtypeStruct((128, 1024), F32)
    moved, gradient = pl.pallas_call(
        kernel,
        out_shape=(block, block),
        in_specs=[hbm, hbm, hbm, hbm, vmem, pl.BlockSpec(memory_space=pltpu.SMEM)],
        out_specs=(hbm, hbm),
        scratch_shapes=[
            pltpu.VMEM((8, 1536, 256), BF16),
            pltpu.VMEM((4, 1536, 256), BF16),
            pltpu.VMEM((2, 2, 4, 8, 128, 128), F32),
            pltpu.VMEM((2, 4, 8, 128, 128), F32),
            pltpu.VMEM((6, 2, 128, 128), F32),
            pltpu.VMEM((2, 6, 2, 128, 128), F32),
            pltpu.VMEM((6, 128, 128), F32),
            pltpu.VMEM((4, 2, 128, 128), F32),
            pltpu.VMEM((2, 128, 128), F32),
            pltpu.VMEM((2, 2, 128, 128), F32),
            pltpu.VMEM((128, 1024), F32),
            pltpu.VMEM((128, 1024), F32),
            pltpu.VMEM((128, 1024), F32),
            pltpu.VMEM((128, 1024), F32),
            pltpu.VMEM((16, 8, 1024), F32),
            pltpu.VMEM((16, 8, 1024), F32),
            pltpu.VMEM((512, 128), F32),
            pltpu.VMEM((2, 3, 8, 128), F32),
            pltpu.VMEM((2, 15, 8, 128), F32),
            pltpu.VMEM((2, 15, 8, 128), F32),
            pltpu.VMEM((8, 128), F32),
            pltpu.VMEM((16, 8, 128), F32),
            pltpu.VMEM((4, 16, 128), F32),
            pltpu.VMEM((2, 4, 32, 128), F32),
            dma((14,)),
            dma((10,)), dma((10,)),
            dma((6,)), dma((6,)),
            dma((2, 6)), dma((2, 6)),
            dma((6,)), dma((6,)),
            dma((4,)), dma((4,)),
            dma((2,)), dma((2,)),
            dma((2, 2)), dma((2, 2)),
            dma((8,)), dma((8,)),
            dma((1,)), dma((1,)),
            dma((2, 2)), dma((2, 2)),
            dma((2,)), dma((2,)),
            dma((1,)),
            pltpu.SemaphoreType.REGULAR((4,)),
        ],
        compiler_params=pltpu.CompilerParams(
            collective_id=0, has_side_effects=True, vmem_limit_bytes=56 * 1024 * 1024
        ),
    )(inputs[0], cotangent[0], weights[0], momentum[0], mix_weights, clip_radius)
    velocity = 0.5 * momentum[0] + gradient
    new = (weights[0] - LEARNING_RATE * velocity) + moved
    return (new[None], velocity[None])


def solution(mesh):
    placed = (
        P("worker", "tok", None),
        P("worker", "tok", None),
        P("worker", "tok", None),
        P("worker", "tok", None),
        P("worker", None),
        P(),
    )
    return jax.shard_map(
        per_device,
        mesh=mesh,
        in_specs=placed,
        out_specs=(P("worker", "tok", None), P("worker", "tok", None)),
        check_vma=False,
    )
```
